32 devices in a mesh: clips: 2 (over y), ha: 8 (over z, x), wa: 2 (over core).
Axes of the slice: x: 2, y: 2, z: 4, core: 2. Of those that a mesh axis runs over, the one named last changes fastest.
Arguments:
- tokens: bfloat16 [5120, 5120], P(('clips', 'ha', 'wa')), parts along dimension 0, may hold values from -640 to 640
- timestep: int32 [2], P('clips'), parts along dimension 0, may hold values from 0 to 49
- time_table: float32 [50, 5120], replicated, may hold values from -3 to 3
- modulation: float32 [2, 5120], replicated, may hold values from -3 to 3
- head_weight: bfloat16 [5120, 64], replicated, may hold values from -0.078125 to 0.078125
- head_bias: float32 [64], replicated, may hold values from -3 to 3
- latent_std: float32 [16], replicated, may hold values from 0.5 to 2
- latent_mean: float32 [16], replicated, may hold values from -3 to 3
- conv_in_weight: bfloat16 [432, 384], replicated, may hold values from -0.3125 to 0.3125
- conv_in_bias: float32 [384], replicated, may hold values from -3 to 3
- norm_gain: float32 [384], replicated, may hold values from 0.1 to 1.9
- conv_weight: bfloat16 [10368, 384], P(None, 'wa'), may hold values from -0.0625 to 0.0625
- conv_bias: float32 [384], replicated, may hold values from -3 to 3
Outputs:
- block_input: bfloat16 [8, 16, 160, 384], P('clips', 'ha', 'wa'), parts along dimension 0
- block_mid: bfloat16 [8, 16, 160, 384], P('clips', 'ha', 'wa'), parts along dimension 0
The draws below stay inside these ranges and needn't reach their ends.
There are 2 independent parts, one for each index of `clips`. The reference program is written for one: setup_inputs(seed, part) draws one part's arguments, and reference() takes and returns one part's arrays. A program takes and returns all parts, laid end to end along the dimension named above; an argument that names none is the same for every part. Nothing has to cross between parts.
All inputs are finite; a program needn't handle non-finite values.
Results may differ from the reference program's by a relative error of at most 0.0058.
Values may be sent and summed in bfloat16 or wider, within the bound.
A program may use at most 128 MiB of HBM per device.

```python
import math
import jax
import jax.numpy as jnp
from jax import lax

D = 5120
ZCH = 16
C = 384
STEPS = 50
F = 4
OUTW = 64
HP = 8
WP = 80
SEQ = 2560


def draw_tokens(key, part):
    keys = jax.random.split(jax.random.fold_in(key, 7), 4)
    rows_scale = jnp.exp(jax.random.uniform(keys[0], (SEQ, 1), jnp.float32, 0.0, math.log(10.0)))
    column_scale = jnp.exp(jax.random.uniform(keys[1], (1, D), jnp.float32, 0.0, math.log(10.0)))
    row_centre = jnp.clip(jax.random.normal(keys[2], (SEQ, 1), jnp.float32), -3.0, 3.0)
    basis = jnp.clip(jax.random.normal(keys[3], (SEQ, D), jnp.float32), -6.0, 6.0)
    values = (basis * column_scale + row_centre) * rows_scale
    return values.astype(jnp.bfloat16)


def steps_of(stream_key, shape, cuts, smallest, top_value):
    level = 1.0
    for axis_at, parts in cuts:
        heights = jax.random.uniform(jax.random.fold_in(jax.random.fold_in(stream_key, 6), axis_at), (parts,), jnp.float32, smallest / len(cuts), top_value / len(cuts))
        level = level * jnp.repeat(jnp.exp(heights), shape[axis_at] // parts).reshape((-1,) + (1,) * (len(shape) - 1 - axis_at))
    return level


def bell_draw(key, dims, scale, bound, shards=(), held_as=jnp.bfloat16):
    gain = steps_of(key, dims, shards, -0.22, 0.18) if shards else 1.0
    entries = jax.random.normal(key, dims, jnp.float32) * scale * gain
    return jnp.minimum(jnp.maximum(entries, -bound), bound).astype(held_as)


def setup_inputs(seed: int = 0, part: int = 0) -> dict:
    splits = jax.random.split(jax.random.key(seed), 14)
    own_keys = jax.random.split(jax.random.fold_in(splits[13], part), 14)
    tokens = draw_tokens(jax.random.fold_in(jax.random.fold_in(splits[13], part), 71), part)
    timestep = jax.random.randint(own_keys[1], (1,), 0, STEPS).astype(jnp.int32)
    time_table = bell_draw(splits[2], (STEPS, D), 0.5, 3.0, (), jnp.float32)
    modulation = bell_draw(splits[3], (2, D), 0.5, 3.0, (), jnp.float32)
    head_weight = bell_draw(splits[4], (D, OUTW), D ** -0.5, 0.078125)
    head_bias = bell_draw(splits[5], (OUTW,), 0.5, 3.0, (), jnp.float32)
    latent_std = jnp.clip(jnp.exp(jax.random.uniform(splits[6], (ZCH,), jnp.float32, math.log(0.5), math.log(2.0))), 0.5, 2.0)
    latent_mean = bell_draw(splits[7], (ZCH,), 0.5, 3.0, (), jnp.float32)
    conv_in_weight = bell_draw(splits[8], (27 * ZCH, C), (27 * ZCH) ** -0.5, 0.3125)
    conv_in_bias = bell_draw(splits[9], (C,), 0.5, 3.0, (), jnp.float32)
    norm_gain = jnp.clip(1.0 + 0.18 * jax.random.normal(splits[10], (C,), jnp.float32), 0.1, 1.9)
    conv_weight = bell_draw(splits[11], (27 * C, C), (27 * C) ** -0.5, 0.0625, ((1, 2),))
    conv_bias = bell_draw(splits[12], (C,), 0.5, 3.0, (), jnp.float32)
    return dict(tokens=tokens, timestep=timestep, time_table=time_table, modulation=modulation, head_weight=head_weight, head_bias=head_bias, latent_std=latent_std, latent_mean=latent_mean, conv_in_weight=conv_in_weight, conv_in_bias=conv_in_bias, norm_gain=norm_gain, conv_weight=conv_weight, conv_bias=conv_bias)


def head_latent(tokens, timestep, time_table, modulation, head_weight, head_bias, latent_std, latent_mean):
    select = jnp.arange(time_table.shape[0], dtype=jnp.int32) == timestep[0]
    embed = lax.optimization_barrier(jnp.sum(jnp.where(select[:, None], time_table, jnp.zeros_like(time_table)), axis=0))
    shift_row = modulation[0] + embed
    scale_row = modulation[1] + embed
    values = tokens.astype(jnp.float32)
    centre = lax.optimization_barrier(jnp.mean(values, axis=-1, keepdims=True))
    spread = lax.optimization_barrier(jnp.mean(jnp.square(values - centre), axis=-1, keepdims=True))
    normed = (values - centre) * lax.rsqrt(spread + 1e-06)
    modded = (normed * (1.0 + scale_row) + shift_row).astype(jnp.bfloat16)
    projected = jnp.dot(modded, head_weight, preferred_element_type=jnp.float32) + head_bias
    repeats = head_weight.shape[1] // latent_std.shape[0]
    return (projected * jnp.tile(latent_std, repeats) + jnp.tile(latent_mean, repeats)).astype(jnp.bfloat16)

def unpatch(flattened, frame_count, row_count, col_count, channels):
    blocks = flattened.reshape(frame_count, row_count, col_count, 2, 2, channels)
    blocks = jnp.transpose(blocks, (0, 1, 3, 2, 4, 5))
    return blocks.reshape(frame_count, row_count * 2, col_count * 2, channels)

def conv_input(region, weight, bias):
    frame_count = region.shape[0] - 2
    row_count = region.shape[1] - 2
    col_count = region.shape[2] - 2
    windows = []
    for time_off in range(3):
        for row_off in range(3):
            for col_off in range(3):
                windows.append(region[time_off:time_off + frame_count, row_off:row_off + row_count, col_off:col_off + col_count])
    stacked = jnp.concatenate(windows, axis=-1).reshape(frame_count * row_count * col_count, -1)
    result = jnp.dot(stacked, weight, preferred_element_type=jnp.float32) + bias
    return result.astype(jnp.bfloat16).reshape(frame_count, row_count, col_count, -1)

def activate(block_input, norm_gain):
    values = block_input.astype(jnp.float32)
    factor = lax.rsqrt(lax.optimization_barrier(jnp.mean(values * values, axis=-1, keepdims=True)) + 1e-06)
    return jax.nn.silu(values * factor * norm_gain).astype(jnp.bfloat16)

def conv_taps(padded, weight):
    batches = padded.shape[0]
    frame_count = padded.shape[1] - 2
    row_count = padded.shape[2] - 2
    col_count = padded.shape[3] - 2
    in_width = padded.shape[4]
    running = jnp.zeros((batches * frame_count * row_count * col_count, weight.shape[1]), jnp.float32)
    for kernel_tap in range(27):
        time_off = kernel_tap // 9
        row_off = kernel_tap // 3 % 3
        col_off = kernel_tap % 3
        window = padded[:, time_off:time_off + frame_count, row_off:row_off + row_count, col_off:col_off + col_count].reshape(-1, in_width)
        running = running + jnp.dot(window, weight[kernel_tap * in_width:(kernel_tap + 1) * in_width], preferred_element_type=jnp.float32)
    return running.reshape(batches, frame_count, row_count, col_count, weight.shape[1])

def reference(tokens, timestep, time_table, modulation, head_weight, head_bias, latent_std, latent_mean, conv_in_weight, conv_in_bias, norm_gain, conv_weight, conv_bias):
    latent_rows = head_latent(tokens, timestep, time_table, modulation, head_weight, head_bias, latent_std, latent_mean)
    latent_image = unpatch(latent_rows, F, HP, WP, latent_std.shape[0])
    padded = jnp.pad(latent_image, ((2, 0), (1, 1), (1, 1), (0, 0)))
    block_input = conv_input(padded, conv_in_weight, conv_in_bias)
    activated = activate(block_input, norm_gain)
    act_padded = jnp.pad(activated, ((2, 0), (1, 1), (1, 1), (0, 0)))
    block_mid = (conv_taps(act_padded[None], conv_weight)[0] + conv_bias).astype(jnp.bfloat16)
    return (block_input, block_mid)
```

```python
import functools

import jax
import jax.numpy as jnp
from jax import lax
from jax.experimental import pallas as pl
from jax.experimental.pallas import tpu as pltpu
from jax.sharding import PartitionSpec as P

F = 4
MESH = pl.DeviceIdType.MESH
CP = 48
F32 = jnp.float32
BF16 = jnp.bfloat16
CHUNK = 32


def dot_t(lhs, rhs):
    return lax.dot_general(lhs, rhs, (((1,), (1,)), ((), ())), preferred_element_type=F32)


def prepare(
    heights,
    widths,
    tok_hbm,
    ts_hbm,
    table_hbm,
    mod_hbm,
    hw_hbm,
    hb_hbm,
    std_hbm,
    mean_hbm,
    ciw_hbm,
    cib_hbm,
    gain_hbm,
    w_hbm,
    act,
    w_ref,
    blk,
    tok,
    ts_ref,
    table_ref,
    mod_ref,
    hw_ref,
    hb_ref,
    std_ref,
    mean_ref,
    ciw_ref,
    cib_ref,
    gain_ref,
    modded,
    strip,
    lat,
    recv,
    zbuf,
    pair,
    wc,
    ybuf,
    xbuf,
    stage,
    tok_sem,
    in_sem,
    send_sem,
    recv_sem,
    w_sem,
):
    ha = lax.axis_index("ha")
    wa = lax.axis_index("wa")
    me = ha * widths + wa
    quarter = heights * widths // F
    frame = me // quarter
    pp = me % quarter
    rows = tok.shape[0]
    cols = rows // 2
    pw = cols // widths
    chan = gain_ref.shape[1]
    half_chan = w_hbm.shape[0]
    zch = std_ref.shape[1]
    odd = ha % 2

    def tok_copy(i):
        part = pl.ds(pl.multiple_of(i * CHUNK, CHUNK), CHUNK)
        return pltpu.make_async_copy(tok_hbm.at[part], tok.at[part], tok_sem.at[i])

    my_half = pl.ds(pl.multiple_of(wa * half_chan, 64), half_chan)
    ts_copy = pltpu.make_async_copy(ts_hbm, ts_ref, in_sem.at[0])
    table_copy = pltpu.make_async_copy(table_hbm, table_ref, in_sem.at[1])
    mod_copy = pltpu.make_async_copy(mod_hbm, mod_ref, in_sem.at[2])
    hw_copy = pltpu.make_async_copy(hw_hbm, hw_ref, in_sem.at[3])
    hb_copy = pltpu.make_async_copy(hb_hbm, hb_ref.at[0], in_sem.at[4])
    std_copy = pltpu.make_async_copy(std_hbm, std_ref.at[0], in_sem.at[5])
    mean_copy = pltpu.make_async_copy(mean_hbm, mean_ref.at[0], in_sem.at[6])
    ciw_copy = pltpu.make_async_copy(ciw_hbm, ciw_ref, in_sem.at[7])
    cib_copy = pltpu.make_async_copy(cib_hbm, cib_ref.at[0], in_sem.at[8])
    gain_copy = pltpu.make_async_copy(gain_hbm, gain_ref.at[0], in_sem.at[9])
    w_copy = pltpu.make_async_copy(w_hbm, w_ref.at[my_half], in_sem.at[10])
    w_send = pltpu.make_async_remote_copy(
        src_ref=w_hbm,
        dst_ref=w_ref.at[my_half],
        send_sem=w_sem.at[0],
        recv_sem=w_sem.at[1],
        device_id={"wa": 1 - wa},
        device_id_type=MESH,
    )
    ts_copy.start()
    mod_copy.start()
    table_copy.start()
    for i in range(rows // CHUNK):
        tok_copy(i).start()
    for copy in (hw_copy, hb_copy, std_copy, mean_copy):
        copy.start()
    for copy in (ciw_copy, cib_copy, gain_copy, w_copy):
        copy.start()

    def source(ff, kind):
        if kind == 0:
            return ff * quarter + ha // 2, ha >= 0
        beside = ha + 2 * odd - 1
        return ff * quarter + ha // 2 + 2 * odd - 1, (beside >= 0) & (beside < heights)

    @pl.when((ha == 0) | (ha == heights - 1))
    def _():
        for ff in range(F):
            recv[ff, 1] = jnp.zeros(recv.shape[2:], BF16)

    barrier = pltpu.get_barrier_semaphore()
    for ff in range(F):
        for kind in range(2):
            device, exists = source(ff, kind)

            @pl.when(exists & (device != me))
            def _():
                pl.semaphore_signal(
                    barrier,
                    inc=1,
                    device_id={"ha": device // widths, "wa": device % widths},
                    device_id_type=MESH,
                )

    pl.semaphore_signal(barrier, inc=1, device_id={"wa": 1 - wa}, device_id_type=MESH)

    ts_copy.wait()
    mod_copy.wait()
    table_copy.wait()
    embed = table_ref[pl.ds(ts_ref[0], 1), :]
    shift = mod_ref[0:1, :] + embed
    scale = 1.0 + (mod_ref[1:2, :] + embed)

    def head_step(i, carry):
        tok_copy(i).wait()
        for j in range(CHUNK // 16):
            part = pl.ds(pl.multiple_of(i * CHUNK + j * 16, 16), 16)
            values = tok[part, :].astype(F32)
            centre = jnp.mean(values, axis=-1, keepdims=True)
            delta = values - centre
            spread = jnp.mean(delta * delta, axis=-1, keepdims=True)
            modded[part, :] = (delta * lax.rsqrt(spread + 1e-06) * scale + shift).astype(BF16)
        return carry

    lax.fori_loop(0, rows // CHUNK, head_step, 0)
    for copy in (hw_copy, hb_copy, std_copy, mean_copy):
        copy.wait()
    projected = dot_t(modded[...], hw_ref[...]) + hb_ref[...]
    repeats = hw_ref.shape[0] // zch
    projected = projected * jnp.concatenate([std_ref[...]] * repeats, axis=1) + jnp.concatenate(
        [mean_ref[...]] * repeats, axis=1
    )
    strip[0:8, :] = jnp.zeros((8, 128), F32)
    strip[8 : 8 + cols, :] = jnp.concatenate([projected[0:cols], projected[cols:rows]], axis=1)
    strip[8 + cols :, :] = jnp.zeros((strip.shape[0] - 8 - cols, 128), F32)
    for side in range(widths):
        lat[side] = strip[7 + side * pw : 7 + side * pw + CP, :].astype(BF16)

    def targets():
        for k in range(4):
            for side in range(widths):
                to_ha = 2 * pp - 1 + k
                valid = (to_ha >= 0) & (to_ha < heights)
                mine = (to_ha == ha) & (wa == side)
                kind = 0 if k in (1, 2) else 1
                copy = pltpu.make_async_remote_copy(
                    src_ref=lat.at[side],
                    dst_ref=recv.at[frame, kind],
                    send_sem=send_sem.at[k, side],
                    recv_sem=recv_sem.at[frame, kind],
                    device_id={"ha": to_ha, "wa": side},
                    device_id_type=MESH,
                )
                yield valid, mine, copy, side, kind

    expected = jnp.int32(1)
    for k in range(4):
        for side in range(widths):
            to_ha = 2 * pp - 1 + k
            valid = (to_ha >= 0) & (to_ha < heights)
            mine = (to_ha == ha) & (wa == side)
            expected += jnp.where(valid & jnp.logical_not(mine), 1, 0)
    pl.semaphore_wait(barrier, expected)
    for valid, mine, copy, side, kind in targets():

        @pl.when(valid & jnp.logical_not(mine))
        def _():
            copy.start()

        @pl.when(valid & mine)
        def _():
            recv[frame, kind] = lat[side]

    w_send.start()

    for copy in (ciw_copy, cib_copy, gain_copy):
        copy.wait()
    wc[...] = jnp.zeros(wc.shape, BF16)
    for a in range(3):
        for win_row in range(4):
            for win_col in range(4):
                k0 = a * 256 + (win_col // 2) * 128 + (win_row // 2) * 64
                k0 += ((win_row % 2) * 2 + win_col % 2) * zch
                for o_row in range(2):
                    for o_col in range(2):
                        b, e = win_row - o_row, win_col - o_col
                        if 0 <= b < 3 and 0 <= e < 3:
                            r0 = ((3 * a + b) * 3 + e) * zch
                            c0 = (o_row * 2 + o_col) * chan
                            wc[k0 : k0 + zch, c0 : c0 + chan] = ciw_ref[r0 : r0 + zch, :]

    zbuf[...] = jnp.zeros(zbuf.shape, F32)
    lane = lax.broadcasted_iota(jnp.int32, (CP, 128), 1)
    own_lane = (lane < 64) ^ (odd == 1)
    position = lax.broadcasted_iota(jnp.int32, (CP, 1), 0)
    bias_in = jnp.concatenate([cib_ref[...]] * 4, axis=1)
    gain = gain_ref[...]

    for ff in range(F):
        for kind in range(2):
            device, exists = source(ff, kind)

            @pl.when(exists & (device != me))
            def _():
                pltpu.make_async_remote_copy(
                    src_ref=lat.at[0],
                    dst_ref=recv.at[ff, kind],
                    send_sem=send_sem.at[0, 0],
                    recv_sem=recv_sem.at[ff, kind],
                    device_id={"wa": 1 - wa},
                    device_id_type=MESH,
                ).wait_recv()

        near = recv[ff, 0].astype(F32)
        mixed = jnp.where(own_lane, near, recv[ff, 1].astype(F32))
        mixed = jnp.concatenate([mixed[:, 64:128], mixed[:, 0:64]], axis=1)
        for i in range(2):
            dense = jnp.where(odd == 1 - i, near, mixed)
            zbuf[i, 0:CP, :] = dense
            pair[ff, i, :, 0:128] = dense.astype(BF16)
            pair[ff, i, :, 128:256] = zbuf[i, 1 : 1 + CP, :].astype(BF16)

        pieces = [pair[ff + a - 2].reshape(2 * CP, 256) for a in range(max(0, 2 - ff), 3)]
        lhs = jnp.concatenate(pieces, axis=1)
        ybuf[...] = (
            (
                jnp.dot(lhs, wc[wc.shape[0] - lhs.shape[1] :, :], preferred_element_type=F32)
                + bias_in
            )
            .astype(BF16)
            .astype(F32)
        )
        for i in range(2):
            for o_row in range(2):
                row = 2 * i + o_row
                for o_col in range(2):
                    c0 = (o_row * 2 + o_col) * chan
                    v = ybuf[i * CP : (i + 1) * CP, c0 : c0 + chan]
                    factor = lax.rsqrt(jnp.mean(v * v, axis=-1, keepdims=True) + 1e-06)
                    half = v * (0.5 * factor) * gain
                    s = half * jnp.tanh(half) + half
                    if o_col == 0:
                        keep = (position > 0) | (wa > 0)
                    else:
                        keep = (position < pw) | (wa < widths - 1)
                    if row == 0:
                        keep = keep & (ha > 0)
                    if row == 3:
                        keep = keep & (ha < heights - 1)
                    xbuf[o_col] = jnp.where(keep, s, 0.0)
                x0 = xbuf[0, 0:pw, :]
                x1 = xbuf[1, 0:pw, :]
                x0s = xbuf[0, 1 : 1 + pw, :]
                x1s = xbuf[1, 1 : 1 + pw, :]
                act[ff, row, :, 0:chan] = jnp.concatenate([x0, x1], axis=0).astype(BF16)
                act[ff, row, :, chan : 2 * chan] = jnp.concatenate([x1, x0s], axis=0).astype(BF16)
                act[ff, row, :, 2 * chan : 3 * chan] = jnp.concatenate([x0s, x1s], axis=0).astype(
                    BF16
                )
                if row in (1, 2):
                    c0 = o_row * 2 * chan
                    c1 = c0 + chan
                    r0 = i * CP
                    even = ybuf[r0 : r0 + pw, c1 : c1 + chan]
                    after = ybuf[r0 + 1 : r0 + 1 + pw, c0:c1]
                    for q in range(chan // 128):
                        part = slice(q * 128, q * 128 + 128)
                        stage[q, pl.ds(0, pw, stride=2), :] = even[:, part]
                        stage[q, pl.ds(1, pw, stride=2), :] = after[:, part]
                        blk[ff, row - 1, :, part] = stage[q].astype(BF16)

    for valid, mine, copy, side, kind in targets():

        @pl.when(valid & jnp.logical_not(mine))
        def _():
            copy.wait_send()

    w_copy.wait()
    w_send.wait()


def convolve(act, w_ref, blk, cb_ref, out1, out2, acc, stage, res, sem):
    frames, _, cols, depth = act.shape
    chan = w_ref.shape[0]
    pw = cols // 2
    shortcut = pltpu.make_async_copy(blk, out1, sem.at[0])
    shortcut.start()
    block = 2 * cols
    split = 256
    rest = chan - split

    def lhs(count):
        parts = [act[0:count, b : b + 2].reshape(count * block, depth) for b in range(3)]
        return jnp.concatenate(parts, axis=1)

    def taps(a, lo, hi):
        return w_ref[lo:hi, 3 * a * depth : 3 * (a + 1) * depth]

    acc[:, 0:split] = dot_t(lhs(4), taps(2, 0, split))
    both = dot_t(lhs(4), jnp.concatenate([taps(2, split, chan), taps(1, 0, rest)], axis=0))
    acc[:, split:chan] = both[:, 0:rest]
    acc[block:, 0:rest] += both[0 : 3 * block, rest : 2 * rest]
    acc[block:, rest:chan] += dot_t(lhs(3), taps(1, rest, chan))
    acc[2 * block :, 0:split] += dot_t(lhs(2), taps(0, 0, split))
    acc[2 * block :, split:chan] += dot_t(lhs(2), taps(0, split, chan))
    bias = cb_ref[...].reshape(1, chan)
    copies = [shortcut]
    for ff in range(frames):
        for row in range(2):
            r0 = (2 * ff + row) * cols
            full = acc[r0 : r0 + cols, :] + bias
            for q in range(chan // 128):
                part = slice(q * 128, q * 128 + 128)
                stage[q, pl.ds(0, pw, stride=2), :] = full[0:pw, part]
                stage[q, pl.ds(1, pw, stride=2), :] = full[pw:cols, part]
                res[ff, row, :, part] = stage[q].astype(BF16)
        copy = pltpu.make_async_copy(res.at[ff], out2.at[ff], sem.at[1 + ff])
        copy.start()
        copies.append(copy)
    for copy in copies:
        copy.wait()


def shards(
    tokens,
    timestep,
    time_table,
    modulation,
    head_weight,
    head_bias,
    latent_std,
    latent_mean,
    conv_in_weight,
    conv_in_bias,
    norm_gain,
    conv_weight,
    conv_bias,
):
    heights = lax.axis_size("ha")
    widths = lax.axis_size("wa")
    rows, width = tokens.shape
    cols = rows // 2
    chan = norm_gain.shape[0]
    hbm = pl.BlockSpec(memory_space=pltpu.HBM)
    vmem = pl.BlockSpec(memory_space=pltpu.VMEM)
    out = jax.ShapeDtypeStruct((F, 2, cols, chan), BF16)
    inner = pl.pallas_call(
        functools.partial(prepare, heights, widths),
        out_shape=(
            pltpu.VMEM((F, 4, cols, 3 * chan), BF16),
            pltpu.VMEM((chan, conv_weight.shape[0]), BF16),
            pltpu.VMEM((F, 2, cols, chan), BF16),
        ),
        in_specs=[hbm] * 12,
        out_specs=(vmem, vmem, vmem),
        scratch_shapes=[
            pltpu.VMEM((rows, width), BF16),
            pltpu.SMEM((1,), jnp.int32),
            pltpu.VMEM(time_table.shape, F32),
            pltpu.VMEM(modulation.shape, F32),
            pltpu.VMEM(head_weight.shape[::-1], BF16),
            pltpu.VMEM((1,) + head_bias.shape, F32),
            pltpu.VMEM((1,) + latent_std.shape, F32),
            pltpu.VMEM((1,) + latent_mean.shape, F32),
            pltpu.VMEM(conv_in_weight.shape, BF16),
            pltpu.VMEM((1, chan), F32),
            pltpu.VMEM((1, chan), F32),
            pltpu.VMEM((rows, width), BF16),
            pltpu.VMEM((cols + 24, 128), F32),
            pltpu.VMEM((widths, CP, 128), BF16),
            pltpu.VMEM((F, 2, CP, 128), BF16),
            pltpu.VMEM((2, CP + 8, 128), F32),
            pltpu.VMEM((F, 2, CP, 256), BF16),
            pltpu.VMEM((768, 4 * chan), BF16),
            pltpu.VMEM((2 * CP, 4 * chan), F32),
            pltpu.VMEM((2, CP, chan), F32),
            pltpu.VMEM((chan // 128, cols, 128), F32),
            pltpu.SemaphoreType.DMA((rows // CHUNK,)),
            pltpu.SemaphoreType.DMA((11,)),
            pltpu.SemaphoreType.DMA((4, widths)),
            pltpu.SemaphoreType.DMA((F, 2)),
            pltpu.SemaphoreType.DMA((2,)),
        ],
        compiler_params=pltpu.CompilerParams(
            collective_id=0, has_side_effects=True, vmem_limit_bytes=48 << 20
        ),
    )(
        tokens,
        timestep,
        time_table,
        modulation,
        head_weight.T,
        head_bias,
        latent_std,
        latent_mean,
        conv_in_weight,
        conv_in_bias,
        norm_gain,
        conv_weight.T,
    )
    return tuple(
        pl.pallas_call(
            convolve,
            out_shape=(out, out),
            in_specs=[vmem] * 4,
            out_specs=(hbm, hbm),
            scratch_shapes=[
                pltpu.VMEM((F * 2 * cols, chan), F32),
                pltpu.VMEM((chan // 128, cols, 128), F32),
                pltpu.VMEM((F, 2, cols, chan), BF16),
                pltpu.SemaphoreType.DMA((1 + F,)),
            ],
            compiler_params=pltpu.CompilerParams(vmem_limit_bytes=32 << 20),
        )(*inner, conv_bias)
    )


def solution(mesh):
    in_specs = (
        P(("clips", "ha", "wa"), None),
        P("clips"),
        P(),
        P(),
        P(),
        P(),
        P(),
        P(),
        P(),
        P(),
        P(),
        P(None, "wa"),
        P(),
    )
    out_specs = (P("clips", "ha", "wa", None), P("clips", "ha", "wa", None))
    return jax.shard_map(shards, mesh=mesh, in_specs=in_specs, out_specs=out_specs, check_vma=False)
```

```python
import functools

import jax
import jax.numpy as jnp
from jax import lax
from jax.experimental import pallas as pl
from jax.experimental.pallas import tpu as pltpu
from jax.sharding import PartitionSpec as P

F = 4
MESH = pl.DeviceIdType.MESH
CP = 48
F32 = jnp.float32
BF16 = jnp.bfloat16
CHUNK = 16


def dot_t(lhs, rhs):
    return lax.dot_general(lhs, rhs, (((1,), (1,)), ((), ())), preferred_element_type=F32)


def prepare(
    heights,
    widths,
    tok_hbm,
    ts_hbm,
    table_hbm,
    mod_hbm,
    hw_hbm,
    hb_hbm,
    std_hbm,
    mean_hbm,
    ciw_hbm,
    cib_hbm,
    gain_hbm,
    w_hbm,
    act,
    w_ref,
    blk,
    tok,
    ts_ref,
    table_ref,
    mod_ref,
    hw_ref,
    hb_ref,
    std_ref,
    mean_ref,
    ciw_ref,
    cib_ref,
    gain_ref,
    scaled,
    shifts,
    centred,
    strip,
    lat,
    recv,
    zbuf,
    pair,
    wc,
    ybuf,
    xbuf,
    stage,
    tok_sem,
    in_sem,
    send_sem,
    recv_sem,
    w_sem,
):
    ha = lax.axis_index("ha")
    wa = lax.axis_index("wa")
    me = ha * widths + wa
    quarter = heights * widths // F
    frame = me // quarter
    pp = me % quarter
    rows = tok.shape[0]
    cols = rows // 2
    pw = cols // widths
    chan = gain_ref.shape[1]
    half_chan = w_hbm.shape[0]
    zch = std_ref.shape[1]
    odd = ha % 2

    def tok_copy(i):
        part = pl.ds(pl.multiple_of(i * CHUNK, CHUNK), CHUNK)
        return pltpu.make_async_copy(tok_hbm.at[part], tok.at[part], tok_sem.at[i])

    my_half = pl.ds(pl.multiple_of(wa * half_chan, 64), half_chan)
    ts_copy = pltpu.make_async_copy(ts_hbm, ts_ref, in_sem.at[0])
    table_copy = pltpu.make_async_copy(table_hbm, table_ref, in_sem.at[1])
    mod_copy = pltpu.make_async_copy(mod_hbm, mod_ref, in_sem.at[2])
    hw_copy = pltpu.make_async_copy(hw_hbm, hw_ref, in_sem.at[3])
    hb_copy = pltpu.make_async_copy(hb_hbm, hb_ref.at[0], in_sem.at[4])
    std_copy = pltpu.make_async_copy(std_hbm, std_ref.at[0], in_sem.at[5])
    mean_copy = pltpu.make_async_copy(mean_hbm, mean_ref.at[0], in_sem.at[6])
    ciw_copy = pltpu.make_async_copy(ciw_hbm, ciw_ref, in_sem.at[7])
    cib_copy = pltpu.make_async_copy(cib_hbm, cib_ref.at[0], in_sem.at[8])
    gain_copy = pltpu.make_async_copy(gain_hbm, gain_ref.at[0], in_sem.at[9])
    w_copy = pltpu.make_async_copy(w_hbm, w_ref.at[my_half], in_sem.at[10])
    w_send = pltpu.make_async_remote_copy(
        src_ref=w_hbm,
        dst_ref=w_ref.at[my_half],
        send_sem=w_sem.at[0],
        recv_sem=w_sem.at[1],
        device_id={"wa": 1 - wa},
        device_id_type=MESH,
    )
    for i in range(rows // CHUNK):
        tok_copy(i).start()
    for copy in (ts_copy, mod_copy):
        copy.start()

    def source(ff, kind):
        if kind == 0:
            return ff * quarter + ha // 2, ha >= 0
        beside = ha + 2 * odd - 1
        return ff * quarter + ha // 2 + 2 * odd - 1, (beside >= 0) & (beside < heights)

    @pl.when((ha == 0) | (ha == heights - 1))
    def _():
        for ff in range(F):
            recv[ff, 1] = jnp.zeros(recv.shape[2:], BF16)

    barrier = pltpu.get_barrier_semaphore()
    for ff in range(F):
        for kind in range(2):
            device, exists = source(ff, kind)

            @pl.when(exists & (device != me))
            def _():
                pl.semaphore_signal(
                    barrier,
                    inc=1,
                    device_id={"ha": device // widths, "wa": device % widths},
                    device_id_type=MESH,
                )

    pl.semaphore_signal(barrier, inc=1, device_id={"wa": 1 - wa}, device_id_type=MESH)

    for copy in (hw_copy, table_copy, hb_copy, std_copy, mean_copy):
        copy.start()
    factors = []
    for i in range(rows // CHUNK):
        tok_copy(i).wait()
    for i in range(rows // CHUNK):
        part = slice(i * CHUNK, (i + 1) * CHUNK)
        values = tok[part, :].astype(F32)
        centre = jnp.mean(values, axis=-1, keepdims=True)
        delta = values - centre
        spread = jnp.mean(delta * delta, axis=-1, keepdims=True)
        centred[part, :] = delta.astype(BF16)
        factors.append(lax.rsqrt(spread + 1e-06))

    for copy in (ts_copy, mod_copy, table_copy, hw_copy):
        copy.wait()
    for copy in (ciw_copy, cib_copy, gain_copy, w_copy):
        copy.start()
    embed = table_ref[pl.ds(ts_ref[0], 1), :]
    shift = mod_ref[0:1, :] + embed
    scale = 1.0 + (mod_ref[1:2, :] + embed)
    outw = hw_ref.shape[0]
    for i in range(outw // 16):
        part = slice(i * 16, (i + 1) * 16)
        scaled[part, :] = (hw_ref[part, :].astype(F32) * scale).astype(BF16)
    high = shift.astype(BF16).astype(F32)
    padding = jnp.zeros((14, shift.shape[1]), F32)
    shifts[...] = jnp.concatenate([high, shift - high, padding], axis=0).astype(BF16)
    offset = dot_t(shifts[...], hw_ref[...])
    for copy in (hb_copy, std_copy, mean_copy):
        copy.wait()
    offset = offset[0:1] + offset[1:2] + hb_ref[...]
    repeats = outw // zch
    deviation = jnp.concatenate([std_ref[...]] * repeats, axis=1)
    average = jnp.concatenate([mean_ref[...]] * repeats, axis=1)
    projected = dot_t(centred[...], scaled[...]) * jnp.concatenate(factors, axis=0) + offset
    projected = projected * deviation + average
    strip[0:8, :] = jnp.zeros((8, 128), F32)
    strip[8 : 8 + cols, :] = jnp.concatenate([projected[0:cols], projected[cols:rows]], axis=1)
    strip[8 + cols :, :] = jnp.zeros((strip.shape[0] - 8 - cols, 128), F32)
    for side in range(widths):
        lat[side] = strip[7 + side * pw : 7 + side * pw + CP, :].astype(BF16)

    def targets():
        for k in range(4):
            for side in range(widths):
                to_ha = 2 * pp - 1 + k
                valid = (to_ha >= 0) & (to_ha < heights)
                mine = (to_ha == ha) & (wa == side)
                kind = 0 if k in (1, 2) else 1
                copy = pltpu.make_async_remote_copy(
                    src_ref=lat.at[side],
                    dst_ref=recv.at[frame, kind],
                    send_sem=send_sem.at[k, side],
                    recv_sem=recv_sem.at[frame, kind],
                    device_id={"ha": to_ha, "wa": side},
                    device_id_type=MESH,
                )
                yield k, valid, mine, copy, side, kind

    expected = jnp.int32(1)
    for _, valid, mine, _, _, _ in targets():
        expected += jnp.where(valid & jnp.logical_not(mine), 1, 0)
    pl.semaphore_wait(barrier, expected)
    for k, valid, mine, copy, side, kind in targets():

        @pl.when(valid & jnp.logical_not(mine))
        def _():
            copy.start()

        @pl.when(valid & mine)
        def _():
            recv[frame, kind] = lat[side]

    w_send.start()

    for copy in (ciw_copy, cib_copy, gain_copy):
        copy.wait()
    wc[...] = jnp.zeros(wc.shape, BF16)
    for a in range(3):
        for win_row in range(4):
            for win_col in range(4):
                k0 = a * 256 + (win_col // 2) * 128 + (win_row // 2) * 64
                k0 += ((win_row % 2) * 2 + win_col % 2) * zch
                for o_row in range(2):
                    for o_col in range(2):
                        b, e = win_row - o_row, win_col - o_col
                        if 0 <= b < 3 and 0 <= e < 3:
                            r0 = ((3 * a + b) * 3 + e) * zch
                            c0 = (o_row * 2 + o_col) * chan
                            wc[k0 : k0 + zch, c0 : c0 + chan] = ciw_ref[r0 : r0 + zch, :]

    zbuf[...] = jnp.zeros(zbuf.shape, F32)
    lane = lax.broadcasted_iota(jnp.int32, (CP, 128), 1)
    own_lane = (lane < 64) ^ (odd == 1)
    position = lax.broadcasted_iota(jnp.int32, (CP, 1), 0)
    bias_in = jnp.concatenate([cib_ref[...]] * 4, axis=1)
    gain = gain_ref[...]

    def take(ff):
        for kind in range(2):
            device, exists = source(ff, kind)

            @pl.when(exists & (device != me))
            def _():
                pltpu.make_async_remote_copy(
                    src_ref=lat.at[0],
                    dst_ref=recv.at[ff, kind],
                    send_sem=send_sem.at[0, 0],
                    recv_sem=recv_sem.at[ff, kind],
                    device_id={"wa": 1 - wa},
                    device_id_type=MESH,
                ).wait_recv()

    def windows(ff):
        near = recv[ff, 0].astype(F32)
        mixed = jnp.where(own_lane, near, recv[ff, 1].astype(F32))
        mixed = jnp.concatenate([mixed[:, 64:128], mixed[:, 0:64]], axis=1)
        for i in range(2):
            dense = jnp.where(odd == 1 - i, near, mixed)
            zbuf[i, 0:CP, :] = dense
            pair[ff, i, :, 0:128] = dense.astype(BF16)
            pair[ff, i, :, 128:256] = zbuf[i, 1 : 1 + CP, :].astype(BF16)

    tall = 2 * CP

    def activate(ff):
        base = ff * tall
        for i in range(2):
            for o_row in range(2):
                row = 2 * i + o_row
                for o_col in range(2):
                    c0 = (o_row * 2 + o_col) * chan
                    v = ybuf[base + i * CP : base + (i + 1) * CP, c0 : c0 + chan]
                    factor = lax.rsqrt(jnp.mean(v * v, axis=-1, keepdims=True) + 1e-06)
                    half = v * (0.5 * factor) * gain
                    s = half * jnp.tanh(half) + half
                    if o_col == 0:
                        keep = (position > 0) | (wa > 0)
                    else:
                        keep = (position < pw) | (wa < widths - 1)
                    if row == 0:
                        keep = keep & (ha > 0)
                    if row == 3:
                        keep = keep & (ha < heights - 1)
                    xbuf[o_col] = jnp.where(keep, s, 0.0)
                x0 = xbuf[0, 0:pw, :]
                x1 = xbuf[1, 0:pw, :]
                x0s = xbuf[0, 1 : 1 + pw, :]
                x1s = xbuf[1, 1 : 1 + pw, :]
                act[ff, row, :, 0:chan] = jnp.concatenate([x0, x1], axis=0).astype(BF16)
                act[ff, row, :, chan : 2 * chan] = jnp.concatenate([x1, x0s], axis=0).astype(BF16)
                act[ff, row, :, 2 * chan : 3 * chan] = jnp.concatenate([x0s, x1s], axis=0).astype(
                    BF16
                )
                if row in (1, 2):
                    c0 = o_row * 2 * chan
                    c1 = c0 + chan
                    r0 = base + i * CP
                    even = ybuf[r0 : r0 + pw, c1 : c1 + chan]
                    after = ybuf[r0 + 1 : r0 + 1 + pw, c0:c1]
                    for q in range(chan // 128):
                        part = slice(q * 128, q * 128 + 128)
                        stage[q, pl.ds(0, pw, stride=2), :] = even[:, part]
                        stage[q, pl.ds(1, pw, stride=2), :] = after[:, part]
                        blk[ff, row - 1, :, part] = stage[q].astype(BF16)

    def block_of(ff):
        return pair[ff].reshape(tall, 256)

    def rounded(ff, total):
        ybuf[ff * tall : (ff + 1) * tall, :] = total.astype(BF16).astype(F32)

    def by_taps(lhs, lo):
        return jnp.dot(lhs, wc[lo : lo + lhs.shape[1], :], preferred_element_type=F32)

    take(0)
    windows(0)
    rounded(0, by_taps(block_of(0), 512) + bias_in)
    activate(0)
    take(1)
    windows(1)
    lhs = jnp.concatenate([block_of(0), block_of(1)], axis=1)
    rounded(1, by_taps(lhs, 256) + bias_in)
    activate(1)
    take(2)
    windows(2)
    blank = jnp.zeros((tall, 256), BF16)
    lines = [(block_of(0), block_of(1), block_of(2)), (block_of(1), block_of(2), blank)]
    lhs = jnp.concatenate([jnp.concatenate(line, axis=1) for line in lines], axis=0)
    total = by_taps(lhs, 0) + bias_in
    rounded(2, total[0:tall])
    ybuf[3 * tall :, :] = total[tall:]
    activate(2)
    take(3)
    windows(3)
    rounded(3, ybuf[3 * tall :, :] + by_taps(block_of(3), 512))
    activate(3)

    for _, valid, mine, copy, _, _ in targets():

        @pl.when(valid & jnp.logical_not(mine))
        def _():
            copy.wait_send()

    w_copy.wait()
    w_send.wait()


def convolve(act, w_ref, blk, cb_ref, out1, out2, acc, stage, res, sem):
    frames, _, cols, depth = act.shape
    chan = w_ref.shape[0]
    pw = cols // 2
    shortcut = pltpu.make_async_copy(blk, out1, sem.at[0])
    shortcut.start()
    block = 2 * cols
    split = 256
    rest = chan - split

    def lhs(count):
        parts = [act[0:count, b : b + 2].reshape(count * block, depth) for b in range(3)]
        return jnp.concatenate(parts, axis=1)

    def taps(a, lo, hi):
        return w_ref[lo:hi, 3 * a * depth : 3 * (a + 1) * depth]

    acc[:, 0:split] = dot_t(lhs(4), taps(2, 0, split))
    both = dot_t(lhs(4), jnp.concatenate([taps(2, split, chan), taps(1, 0, rest)], axis=0))
    acc[:, split:chan] = both[:, 0:rest]
    acc[block:, 0:rest] += both[0 : 3 * block, rest : 2 * rest]
    acc[block:, rest:chan] += dot_t(lhs(3), taps(1, rest, chan))
    acc[2 * block :, 0:split] += dot_t(lhs(2), taps(0, 0, split))
    acc[2 * block :, split:chan] += dot_t(lhs(2), taps(0, split, chan))
    bias = cb_ref[...].reshape(1, chan)
    copies = [shortcut]
    for ff in range(frames):
        for row in range(2):
            r0 = (2 * ff + row) * cols
            full = acc[r0 : r0 + cols, :] + bias
            for q in range(chan // 128):
                part = slice(q * 128, q * 128 + 128)
                stage[q, pl.ds(0, pw, stride=2), :] = full[0:pw, part]
                stage[q, pl.ds(1, pw, stride=2), :] = full[pw:cols, part]
                res[ff, row, :, part] = stage[q].astype(BF16)
        copy = pltpu.make_async_copy(res.at[ff], out2.at[ff], sem.at[1 + ff])
        copy.start()
        copies.append(copy)
    for copy in copies:
        copy.wait()


def shards(
    tokens,
    timestep,
    time_table,
    modulation,
    head_weight,
    head_bias,
    latent_std,
    latent_mean,
    conv_in_weight,
    conv_in_bias,
    norm_gain,
    conv_weight,
    conv_bias,
):
    heights = lax.axis_size("ha")
    widths = lax.axis_size("wa")
    rows, width = tokens.shape
    cols = rows // 2
    chan = norm_gain.shape[0]
    hbm = pl.BlockSpec(memory_space=pltpu.HBM)
    vmem = pl.BlockSpec(memory_space=pltpu.VMEM)
    out = jax.ShapeDtypeStruct((F, 2, cols, chan), BF16)
    inner = pl.pallas_call(
        functools.partial(prepare, heights, widths),
        out_shape=(
            pltpu.VMEM((F, 4, cols, 3 * chan), BF16),
            pltpu.VMEM((chan, conv_weight.shape[0]), BF16),
            pltpu.VMEM((F, 2, cols, chan), BF16),
        ),
        in_specs=[hbm] * 12,
        out_specs=(vmem, vmem, vmem),
        scratch_shapes=[
            pltpu.VMEM((rows, width), BF16),
            pltpu.SMEM((1,), jnp.int32),
            pltpu.VMEM(time_table.shape, F32),
            pltpu.VMEM(modulation.shape, F32),
            pltpu.VMEM(head_weight.shape[::-1], BF16),
            pltpu.VMEM((1,) + head_bias.shape, F32),
            pltpu.VMEM((1,) + latent_std.shape, F32),
            pltpu.VMEM((1,) + latent_mean.shape, F32),
            pltpu.VMEM(conv_in_weight.shape, BF16),
            pltpu.VMEM((1, chan), F32),
            pltpu.VMEM((1, chan), F32),
            pltpu.VMEM(head_weight.shape[::-1], BF16),
            pltpu.VMEM((16, width), BF16),
            pltpu.VMEM((rows, width), BF16),
            pltpu.VMEM((cols + 24, 128), F32),
            pltpu.VMEM((widths, CP, 128), BF16),
            pltpu.VMEM((F, 2, CP, 128), BF16),
            pltpu.VMEM((2, CP + 8, 128), F32),
            pltpu.VMEM((F, 2, CP, 256), BF16),
            pltpu.VMEM((768, 4 * chan), BF16),
            pltpu.VMEM((F * 2 * CP, 4 * chan), F32),
            pltpu.VMEM((2, CP, chan), F32),
            pltpu.VMEM((chan // 128, cols, 128), F32),
            pltpu.SemaphoreType.DMA((rows // CHUNK,)),
            pltpu.SemaphoreType.DMA((11,)),
            pltpu.SemaphoreType.DMA((4, widths)),
            pltpu.SemaphoreType.DMA((F, 2)),
            pltpu.SemaphoreType.DMA((2,)),
        ],
        compiler_params=pltpu.CompilerParams(
            collective_id=0, has_side_effects=True, vmem_limit_bytes=48 << 20
        ),
    )(
        *(
            x if x is timestep else pltpu.with_memory_space_constraint(x, pltpu.HBM)
            for x in (
                tokens,
                timestep,
                time_table,
                modulation,
                head_weight.T,
                head_bias,
                latent_std,
                latent_mean,
                conv_in_weight,
                conv_in_bias,
                norm_gain,
                conv_weight.T,
            )
        )
    )
    return tuple(
        pl.pallas_call(
            convolve,
            out_shape=(out, out),
            in_specs=[vmem] * 4,
            out_specs=(hbm, hbm),
            scratch_shapes=[
                pltpu.VMEM((F * 2 * cols, chan), F32),
                pltpu.VMEM((chan // 128, cols, 128), F32),
                pltpu.VMEM((F, 2, cols, chan), BF16),
                pltpu.SemaphoreType.DMA((1 + F,)),
            ],
            compiler_params=pltpu.CompilerParams(vmem_limit_bytes=32 << 20),
        )(*inner, conv_bias)
    )


def solution(mesh):
    in_specs = (
        P(("clips", "ha", "wa"), None),
        P("clips"),
        P(),
        P(),
        P(),
        P(),
        P(),
        P(),
        P(),
        P(),
        P(),
        P(None, "wa"),
        P(),
    )
    out_specs = (P("clips", "ha", "wa", None), P("clips", "ha", "wa", None))
    return jax.shard_map(shards, mesh=mesh, in_specs=in_specs, out_specs=out_specs, check_vma=False)
```

```python
import functools

import jax
import jax.numpy as jnp
from jax import lax
from jax.experimental import pallas as pl
from jax.experimental.pallas import tpu as pltpu
from jax.sharding import PartitionSpec as P

F = 4
MESH = pl.DeviceIdType.MESH
CP = 48
F32 = jnp.float32
BF16 = jnp.bfloat16
CHUNK = 16


def dot_t(lhs, rhs):
    return lax.dot_general(lhs, rhs, (((1,), (1,)), ((), ())), preferred_element_type=F32)


def prepare(
    heights,
    widths,
    tok_hbm,
    ts_hbm,
    table_hbm,
    mod_hbm,
    hw_hbm,
    hb_hbm,
    std_hbm,
    mean_hbm,
    ciw_hbm,
    cib_hbm,
    gain_hbm,
    w_hbm,
    act,
    w_ref,
    blk,
    tok,
    ts_ref,
    table_ref,
    mod_ref,
    hw_ref,
    hb_ref,
    std_ref,
    mean_ref,
    ciw_ref,
    cib_ref,
    gain_ref,
    scaled,
    shifts,
    centred,
    strip,
    lat,
    recv,
    zbuf,
    pair,
    wc,
    ybuf,
    xbuf,
    stage,
    tok_sem,
    in_sem,
    send_sem,
    recv_sem,
    w_sem,
    turn_sem,
):
    ha = lax.axis_index("ha")
    wa = lax.axis_index("wa")
    me = ha * widths + wa
    quarter = heights * widths // F
    frame = me // quarter
    pp = me % quarter
    rows = tok.shape[0]
    cols = rows // 2
    pw = cols // widths
    chan = gain_ref.shape[1]
    half_chan = w_hbm.shape[0]
    zch = std_ref.shape[1]
    odd = ha % 2

    def tok_copy(i):
        part = pl.ds(pl.multiple_of(i * CHUNK, CHUNK), CHUNK)
        return pltpu.make_async_copy(tok_hbm.at[part], tok.at[part], tok_sem.at[i])

    my_half = pl.ds(pl.multiple_of(wa * half_chan, 64), half_chan)
    ts_copy = pltpu.make_async_copy(ts_hbm, ts_ref, in_sem.at[0])
    table_copy = pltpu.make_async_copy(table_hbm, table_ref, in_sem.at[1])
    mod_copy = pltpu.make_async_copy(mod_hbm, mod_ref, in_sem.at[2])
    hw_copy = pltpu.make_async_copy(hw_hbm, hw_ref, in_sem.at[3])
    hb_copy = pltpu.make_async_copy(hb_hbm, hb_ref.at[0], in_sem.at[4])
    std_copy = pltpu.make_async_copy(std_hbm, std_ref.at[0], in_sem.at[5])
    mean_copy = pltpu.make_async_copy(mean_hbm, mean_ref.at[0], in_sem.at[6])
    ciw_copy = pltpu.make_async_copy(ciw_hbm, ciw_ref, in_sem.at[7])
    cib_copy = pltpu.make_async_copy(cib_hbm, cib_ref.at[0], in_sem.at[8])
    gain_copy = pltpu.make_async_copy(gain_hbm, gain_ref.at[0], in_sem.at[9])
    w_copy = pltpu.make_async_copy(w_hbm, w_ref.at[my_half], in_sem.at[10])
    w_send = pltpu.make_async_remote_copy(
        src_ref=w_hbm,
        dst_ref=w_ref.at[my_half],
        send_sem=w_sem.at[0],
        recv_sem=w_sem.at[1],
        device_id={"wa": 1 - wa},
        device_id_type=MESH,
    )
    for i in range(rows // CHUNK):
        tok_copy(i).start()
    for copy in (ts_copy, mod_copy):
        copy.start()

    def source(ff, kind):
        if kind == 0:
            return ff * quarter + ha // 2, ha >= 0
        beside = ha + 2 * odd - 1
        return ff * quarter + ha // 2 + 2 * odd - 1, (beside >= 0) & (beside < heights)

    @pl.when((ha == 0) | (ha == heights - 1))
    def _():
        for ff in range(F):
            recv[ff, 1] = jnp.zeros(recv.shape[2:], BF16)

    barrier = pltpu.get_barrier_semaphore()
    for ff in range(F):
        for kind in range(2):
            device, exists = source(ff, kind)

            @pl.when(exists & (device != me))
            def _():
                pl.semaphore_signal(
                    barrier,
                    inc=1,
                    device_id={"ha": device // widths, "wa": device % widths},
                    device_id_type=MESH,
                )

    pl.semaphore_signal(barrier, inc=1, device_id={"wa": 1 - wa}, device_id_type=MESH)

    for copy in (hw_copy, table_copy, hb_copy, std_copy, mean_copy):
        copy.start()
    factors = []
    for i in range(rows // CHUNK):
        tok_copy(i).wait()
    for i in range(rows // CHUNK):
        part = slice(i * CHUNK, (i + 1) * CHUNK)
        values = tok[part, :].astype(F32)
        centre = jnp.mean(values, axis=-1, keepdims=True)
        delta = values - centre
        spread = jnp.mean(delta * delta, axis=-1, keepdims=True)
        centred[part, :] = delta.astype(BF16)
        factors.append(lax.rsqrt(spread + 1e-06))

    for copy in (ts_copy, mod_copy, table_copy, hw_copy):
        copy.wait()
    for copy in (ciw_copy, cib_copy, gain_copy, w_copy):
        copy.start()
    embed = table_ref[pl.ds(ts_ref[0], 1), :]
    shift = mod_ref[0:1, :] + embed
    scale = 1.0 + (mod_ref[1:2, :] + embed)
    outw = hw_ref.shape[0]
    for i in range(outw // 16):
        part = slice(i * 16, (i + 1) * 16)
        scaled[part, :] = (hw_ref[part, :].astype(F32) * scale).astype(BF16)
    high = shift.astype(BF16).astype(F32)
    padding = jnp.zeros((14, shift.shape[1]), F32)
    shifts[...] = jnp.concatenate([high, shift - high, padding], axis=0).astype(BF16)
    offset = dot_t(shifts[...], hw_ref[...])
    for copy in (hb_copy, std_copy, mean_copy):
        copy.wait()
    offset = offset[0:1] + offset[1:2] + hb_ref[...]
    repeats = outw // zch
    deviation = jnp.concatenate([std_ref[...]] * repeats, axis=1)
    average = jnp.concatenate([mean_ref[...]] * repeats, axis=1)
    projected = dot_t(centred[...], scaled[...]) * jnp.concatenate(factors, axis=0) + offset
    projected = projected * deviation + average
    strip[0:8, :] = jnp.zeros((8, 128), F32)
    strip[8 : 8 + cols, :] = jnp.concatenate([projected[0:cols], projected[cols:rows]], axis=1)
    strip[8 + cols :, :] = jnp.zeros((strip.shape[0] - 8 - cols, 128), F32)
    for side in range(widths):
        lat[side] = strip[7 + side * pw : 7 + side * pw + CP, :].astype(BF16)

    def targets():
        for k in range(4):
            for side in range(widths):
                to_ha = 2 * pp - 1 + k
                valid = (to_ha >= 0) & (to_ha < heights)
                mine = (to_ha == ha) & (wa == side)
                kind = 0 if k in (1, 2) else 1
                copy = pltpu.make_async_remote_copy(
                    src_ref=lat.at[side],
                    dst_ref=recv.at[frame, kind],
                    send_sem=send_sem.at[k, side],
                    recv_sem=recv_sem.at[frame, kind],
                    device_id={"ha": to_ha, "wa": side},
                    device_id_type=MESH,
                )
                yield k, valid, mine, copy, side, kind

    expected = jnp.int32(1)
    for _, valid, mine, _, _, _ in targets():
        expected += jnp.where(valid & jnp.logical_not(mine), 1, 0)
    pl.semaphore_wait(barrier, expected)
    lead = (frame == F - 1) & (pp == 0)

    @pl.when((frame == F - 1) & (pp == 1))
    def _():
        pl.semaphore_wait(turn_sem, 1)

    for k, valid, mine, copy, side, kind in targets():
        if k == 2 and side == 0:
            @pl.when(lead)
            def _():
                pl.semaphore_signal(
                    turn_sem, inc=1, device_id={"wa": 1 - wa}, device_id_type=MESH
                )

        @pl.when(valid & jnp.logical_not(mine))
        def _():
            copy.start()

        @pl.when(valid & mine)
        def _():
            recv[frame, kind] = lat[side]

    w_send.start()

    for copy in (ciw_copy, cib_copy, gain_copy):
        copy.wait()
    wc[...] = jnp.zeros(wc.shape, BF16)
    for a in range(3):
        for win_row in range(4):
            for win_col in range(4):
                k0 = a * 256 + (win_col // 2) * 128 + (win_row // 2) * 64
                k0 += ((win_row % 2) * 2 + win_col % 2) * zch
                for o_row in range(2):
                    for o_col in range(2):
                        b, e = win_row - o_row, win_col - o_col
                        if 0 <= b < 3 and 0 <= e < 3:
                            r0 = ((3 * a + b) * 3 + e) * zch
                            c0 = (o_row * 2 + o_col) * chan
                            wc[k0 : k0 + zch, c0 : c0 + chan] = ciw_ref[r0 : r0 + zch, :]

    zbuf[...] = jnp.zeros(zbuf.shape, F32)
    lane = lax.broadcasted_iota(jnp.int32, (CP, 128), 1)
    own_lane = (lane < 64) ^ (odd == 1)
    position = lax.broadcasted_iota(jnp.int32, (CP, 1), 0)
    bias_in = jnp.concatenate([cib_ref[...]] * 4, axis=1)
    gain = gain_ref[...]

    def take(ff):
        for kind in range(2):
            device, exists = source(ff, kind)

            @pl.when(exists & (device != me))
            def _():
                pltpu.make_async_remote_copy(
                    src_ref=lat.at[0],
                    dst_ref=recv.at[ff, kind],
                    send_sem=send_sem.at[0, 0],
                    recv_sem=recv_sem.at[ff, kind],
                    device_id={"wa": 1 - wa},
                    device_id_type=MESH,
                ).wait_recv()

    def windows(ff):
        near = recv[ff, 0].astype(F32)
        mixed = jnp.where(own_lane, near, recv[ff, 1].astype(F32))
        mixed = jnp.concatenate([mixed[:, 64:128], mixed[:, 0:64]], axis=1)
        for i in range(2):
            dense = jnp.where(odd == 1 - i, near, mixed)
            zbuf[i, 0:CP, :] = dense
            pair[ff, i, :, 0:128] = dense.astype(BF16)
            pair[ff, i, :, 128:256] = zbuf[i, 1 : 1 + CP, :].astype(BF16)

    tall = 2 * CP

    def activate(ff):
        base = ff * tall
        for i in range(2):
            for o_row in range(2):
                row = 2 * i + o_row
                for o_col in range(2):
                    c0 = (o_row * 2 + o_col) * chan
                    v = ybuf[base + i * CP : base + (i + 1) * CP, c0 : c0 + chan]
                    factor = lax.rsqrt(jnp.mean(v * v, axis=-1, keepdims=True) + 1e-06)
                    half = v * (0.5 * factor) * gain
                    s = half * jnp.tanh(half) + half
                    if o_col == 0:
                        keep = (position > 0) | (wa > 0)
                    else:
                        keep = (position < pw) | (wa < widths - 1)
                    if row == 0:
                        keep = keep & (ha > 0)
                    if row == 3:
                        keep = keep & (ha < heights - 1)
                    xbuf[o_col] = jnp.where(keep, s, 0.0)
                x0 = xbuf[0, 0:pw, :]
                x1 = xbuf[1, 0:pw, :]
                x0s = xbuf[0, 1 : 1 + pw, :]
                x1s = xbuf[1, 1 : 1 + pw, :]
                act[ff, row, :, 0:chan] = jnp.concatenate([x0, x1], axis=0).astype(BF16)
                act[ff, row, :, chan : 2 * chan] = jnp.concatenate([x1, x0s], axis=0).astype(BF16)
                act[ff, row, :, 2 * chan : 3 * chan] = jnp.concatenate([x0s, x1s], axis=0).astype(
                    BF16
                )
                if row in (1, 2):
                    c0 = o_row * 2 * chan
                    c1 = c0 + chan
                    r0 = base + i * CP
                    even = ybuf[r0 : r0 + pw, c1 : c1 + chan]
                    after = ybuf[r0 + 1 : r0 + 1 + pw, c0:c1]
                    for q in range(chan // 128):
                        part = slice(q * 128, q * 128 + 128)
                        stage[q, pl.ds(0, pw, stride=2), :] = even[:, part]
                        stage[q, pl.ds(1, pw, stride=2), :] = after[:, part]
                        blk[ff, row - 1, :, part] = stage[q].astype(BF16)

    def block_of(ff):
        return pair[ff].reshape(tall, 256)

    def rounded(ff, total):
        ybuf[ff * tall : (ff + 1) * tall, :] = total.astype(BF16).astype(F32)

    def by_taps(lhs, lo):
        return jnp.dot(lhs, wc[lo : lo + lhs.shape[1], :], preferred_element_type=F32)

    take(0)
    windows(0)
    rounded(0, by_taps(block_of(0), 512) + bias_in)
    activate(0)
    take(1)
    windows(1)
    lhs = jnp.concatenate([block_of(0), block_of(1)], axis=1)
    rounded(1, by_taps(lhs, 256) + bias_in)
    activate(1)
    take(2)
    windows(2)
    blank = jnp.zeros((tall, 256), BF16)
    lines = [(block_of(0), block_of(1), block_of(2)), (block_of(1), block_of(2), blank)]
    lhs = jnp.concatenate([jnp.concatenate(line, axis=1) for line in lines], axis=0)
    total = by_taps(lhs, 0) + bias_in
    rounded(2, total[0:tall])
    ybuf[3 * tall :, :] = total[tall:]
    activate(2)
    take(3)
    windows(3)
    rounded(3, ybuf[3 * tall :, :] + by_taps(block_of(3), 512))
    activate(3)

    for k, valid, mine, copy, _, _ in targets():
        pending = valid & jnp.logical_not(mine)

        @pl.when(pending)
        def _():
            copy.wait_send()

    w_copy.wait()
    w_send.wait()


def convolve(act, w_ref, blk, cb_ref, out1, out2, acc, stage, res, sem):
    frames, _, cols, depth = act.shape
    chan = w_ref.shape[0]
    pw = cols // 2
    shortcut = pltpu.make_async_copy(blk, out1, sem.at[0])
    shortcut.start()
    block = 2 * cols
    split = 256
    rest = chan - split

    def lhs(count):
        parts = [act[0:count, b : b + 2].reshape(count * block, depth) for b in range(3)]
        return jnp.concatenate(parts, axis=1)

    def taps(a, lo, hi):
        return w_ref[lo:hi, 3 * a * depth : 3 * (a + 1) * depth]

    acc[:, 0:split] = dot_t(lhs(4), taps(2, 0, split))
    both = dot_t(lhs(4), jnp.concatenate([taps(2, split, chan), taps(1, 0, rest)], axis=0))
    acc[:, split:chan] = both[:, 0:rest]
    acc[block:, 0:rest] += both[0 : 3 * block, rest : 2 * rest]
    acc[block:, rest:chan] += dot_t(lhs(3), taps(1, rest, chan))
    bias = cb_ref[...].reshape(1, chan)
    copies = [shortcut]

    def finish(ff):
        for row in range(2):
            r0 = (2 * ff + row) * cols
            full = acc[r0 : r0 + cols, :] + bias
            for q in range(chan // 128):
                part = slice(q * 128, q * 128 + 128)
                stage[q, pl.ds(0, pw, stride=2), :] = full[0:pw, part]
                stage[q, pl.ds(1, pw, stride=2), :] = full[pw:cols, part]
                res[ff, row, :, part] = stage[q].astype(BF16)
        copy = pltpu.make_async_copy(res.at[ff], out2.at[ff], sem.at[1 + ff])
        copy.start()
        copies.append(copy)

    late = dot_t(lhs(2), taps(0, 0, split))
    acc[2 * block :, split:chan] += dot_t(lhs(2), taps(0, split, chan))
    finish(0)
    finish(1)
    acc[2 * block :, 0:split] += late
    finish(2)
    finish(3)
    for copy in copies:
        copy.wait()


def shards(
    tokens,
    timestep,
    time_table,
    modulation,
    head_weight,
    head_bias,
    latent_std,
    latent_mean,
    conv_in_weight,
    conv_in_bias,
    norm_gain,
    conv_weight,
    conv_bias,
):
    heights = lax.axis_size("ha")
    widths = lax.axis_size("wa")
    rows, width = tokens.shape
    cols = rows // 2
    chan = norm_gain.shape[0]
    hbm = pl.BlockSpec(memory_space=pltpu.HBM)
    vmem = pl.BlockSpec(memory_space=pltpu.VMEM)
    out = jax.ShapeDtypeStruct((F, 2, cols, chan), BF16)
    inner = pl.pallas_call(
        functools.partial(prepare, heights, widths),
        out_shape=(
            pltpu.VMEM((F, 4, cols, 3 * chan), BF16),
            pltpu.VMEM((chan, conv_weight.shape[0]), BF16),
            pltpu.VMEM((F, 2, cols, chan), BF16),
        ),
        in_specs=[hbm] * 12,
        out_specs=(vmem, vmem, vmem),
        scratch_shapes=[
            pltpu.VMEM((rows, width), BF16),
            pltpu.SMEM((1,), jnp.int32),
            pltpu.VMEM(time_table.shape, F32),
            pltpu.VMEM(modulation.shape, F32),
            pltpu.VMEM(head_weight.shape[::-1], BF16),
            pltpu.VMEM((1,) + head_bias.shape, F32),
            pltpu.VMEM((1,) + latent_std.shape, F32),
            pltpu.VMEM((1,) + latent_mean.shape, F32),
            pltpu.VMEM(conv_in_weight.shape, BF16),
            pltpu.VMEM((1, chan), F32),
            pltpu.VMEM((1, chan), F32),
            pltpu.VMEM(head_weight.shape[::-1], BF16),
            pltpu.VMEM((16, width), BF16),
            pltpu.VMEM((rows, width), BF16),
            pltpu.VMEM((cols + 24, 128), F32),
            pltpu.VMEM((widths, CP, 128), BF16),
            pltpu.VMEM((F, 2, CP, 128), BF16),
            pltpu.VMEM((2, CP + 8, 128), F32),
            pltpu.VMEM((F, 2, CP, 256), BF16),
            pltpu.VMEM((768, 4 * chan), BF16),
            pltpu.VMEM((F * 2 * CP, 4 * chan), F32),
            pltpu.VMEM((2, CP, chan), F32),
            pltpu.VMEM((chan // 128, cols, 128), F32),
            pltpu.SemaphoreType.DMA((rows // CHUNK,)),
            pltpu.SemaphoreType.DMA((11,)),
            pltpu.SemaphoreType.DMA((4, widths)),
            pltpu.SemaphoreType.DMA((F, 2)),
            pltpu.SemaphoreType.DMA((2,)),
            pltpu.SemaphoreType.REGULAR,
        ],
        compiler_params=pltpu.CompilerParams(
            collective_id=0, has_side_effects=True, vmem_limit_bytes=48 << 20
        ),
    )(
        *(
            x if x is timestep else pltpu.with_memory_space_constraint(x, pltpu.HBM)
            for x in (
                tokens,
                timestep,
                time_table,
                modulation,
                head_weight.T,
                head_bias,
                latent_std,
                latent_mean,
                conv_in_weight,
                conv_in_bias,
                norm_gain,
                conv_weight.T,
            )
        )
    )
    return tuple(
        pl.pallas_call(
            convolve,
            out_shape=(out, out),
            in_specs=[vmem] * 4,
            out_specs=(hbm, hbm),
            scratch_shapes=[
                pltpu.VMEM((F * 2 * cols, chan), F32),
                pltpu.VMEM((chan // 128, cols, 128), F32),
                pltpu.VMEM((F, 2, cols, chan), BF16),
                pltpu.SemaphoreType.DMA((1 + F,)),
            ],
            compiler_params=pltpu.CompilerParams(vmem_limit_bytes=32 << 20),
        )(*inner, conv_bias)
    )


def solution(mesh):
    in_specs = (
        P(("clips", "ha", "wa"), None),
        P("clips"),
        P(),
        P(),
        P(),
        P(),
        P(),
        P(),
        P(),
        P(),
        P(),
        P(None, "wa"),
        P(),
    )
    out_specs = (P("clips", "ha", "wa", None), P("clips", "ha", "wa", None))
    return jax.shard_map(shards, mesh=mesh, in_specs=in_specs, out_specs=out_specs, check_vma=False)
```

```python
import functools

import jax
import jax.numpy as jnp
from jax import lax
from jax.experimental import pallas as pl
from jax.experimental.pallas import tpu as pltpu
from jax.sharding import PartitionSpec as P

F = 4
MESH = pl.DeviceIdType.MESH
CP = 48
F32 = jnp.float32
BF16 = jnp.bfloat16
CHUNK = 32


def dot_t(lhs, rhs):
    return lax.dot_general(lhs, rhs, (((1,), (1,)), ((), ())), preferred_element_type=F32)


def prepare(
    heights,
    widths,
    tok_hbm,
    ts_hbm,
    table_hbm,
    mod_hbm,
    hw_hbm,
    hb_hbm,
    std_hbm,
    mean_hbm,
    ciw_hbm,
    cib_hbm,
    gain_hbm,
    w_hbm,
    act,
    w_ref,
    blk,
    tok,
    ts_ref,
    table_ref,
    mod_ref,
    hw_ref,
    hb_ref,
    std_ref,
    mean_ref,
    ciw_ref,
    cib_ref,
    gain_ref,
    scaled,
    shifts,
    centred,
    strip,
    lat,
    recv,
    zbuf,
    pair,
    wc,
    ybuf,
    xbuf,
    stage,
    tok_sem,
    in_sem,
    send_sem,
    recv_sem,
    w_sem,
    turn_sem,
):
    ha = lax.axis_index("ha")
    wa = lax.axis_index("wa")
    me = ha * widths + wa
    quarter = heights * widths // F
    frame = me // quarter
    pp = me % quarter
    rows = tok.shape[0]
    cols = rows // 2
    pw = cols // widths
    chan = gain_ref.shape[1]
    half_chan = w_hbm.shape[0]
    zch = std_ref.shape[1]
    odd = ha % 2

    def tok_copy(i):
        part = pl.ds(pl.multiple_of(i * CHUNK, CHUNK), CHUNK)
        return pltpu.make_async_copy(tok_hbm.at[part], tok.at[part], tok_sem.at[i])

    my_half = pl.ds(pl.multiple_of(wa * half_chan, 64), half_chan)
    ts_copy = pltpu.make_async_copy(ts_hbm, ts_ref, in_sem.at[0])
    table_copy = pltpu.make_async_copy(table_hbm, table_ref, in_sem.at[1])
    mod_copy = pltpu.make_async_copy(mod_hbm, mod_ref, in_sem.at[2])
    hw_copy = pltpu.make_async_copy(hw_hbm, hw_ref, in_sem.at[3])
    hb_copy = pltpu.make_async_copy(hb_hbm, hb_ref.at[0], in_sem.at[4])
    std_copy = pltpu.make_async_copy(std_hbm, std_ref.at[0], in_sem.at[5])
    mean_copy = pltpu.make_async_copy(mean_hbm, mean_ref.at[0], in_sem.at[6])
    ciw_copy = pltpu.make_async_copy(ciw_hbm, ciw_ref, in_sem.at[7])
    cib_copy = pltpu.make_async_copy(cib_hbm, cib_ref.at[0], in_sem.at[8])
    gain_copy = pltpu.make_async_copy(gain_hbm, gain_ref.at[0], in_sem.at[9])
    w_copy = pltpu.make_async_copy(w_hbm, w_ref.at[my_half], in_sem.at[10])
    w_send = pltpu.make_async_remote_copy(
        src_ref=w_hbm,
        dst_ref=w_ref.at[my_half],
        send_sem=w_sem.at[0],
        recv_sem=w_sem.at[1],
        device_id={"wa": 1 - wa},
        device_id_type=MESH,
    )
    for i in range(rows // CHUNK):
        tok_copy(i).start()
    for copy in (ts_copy, mod_copy):
        copy.start()

    def source(ff, kind):
        if kind == 0:
            return ff * quarter + ha // 2, ha >= 0
        beside = ha + 2 * odd - 1
        return ff * quarter + ha // 2 + 2 * odd - 1, (beside >= 0) & (beside < heights)

    @pl.when((ha == 0) | (ha == heights - 1))
    def _():
        for ff in range(F):
            recv[ff, 1] = jnp.zeros(recv.shape[2:], BF16)

    barrier = pltpu.get_barrier_semaphore()
    for ff in range(F):
        for kind in range(2):
            device, exists = source(ff, kind)

            @pl.when(exists & (device != me))
            def _():
                pl.semaphore_signal(
                    barrier,
                    inc=1,
                    device_id={"ha": device // widths, "wa": device % widths},
                    device_id_type=MESH,
                )

    pl.semaphore_signal(barrier, inc=1, device_id={"wa": 1 - wa}, device_id_type=MESH)

    for copy in (hw_copy, table_copy, hb_copy, std_copy, mean_copy):
        copy.start()
    factors = []
    for i in range(rows // CHUNK):
        tok_copy(i).wait()
    for i in range(rows // CHUNK):
        part = slice(i * CHUNK, (i + 1) * CHUNK)
        values = tok[part, :].astype(F32)
        centre = jnp.mean(values, axis=-1, keepdims=True)
        delta = values - centre
        spread = jnp.mean(delta * delta, axis=-1, keepdims=True)
        centred[part, :] = delta.astype(BF16)
        factors.append(lax.rsqrt(spread + 1e-06))

    for copy in (ts_copy, mod_copy, table_copy, hw_copy):
        copy.wait()
    for copy in (ciw_copy, cib_copy, gain_copy, w_copy):
        copy.start()
    embed = table_ref[pl.ds(ts_ref[0], 1), :]
    shift = mod_ref[0:1, :] + embed
    scale = 1.0 + (mod_ref[1:2, :] + embed)
    outw = hw_ref.shape[0]
    for i in range(outw // 16):
        part = slice(i * 16, (i + 1) * 16)
        scaled[part, :] = (hw_ref[part, :].astype(F32) * scale).astype(BF16)
    high = shift.astype(BF16).astype(F32)
    padding = jnp.zeros((14, shift.shape[1]), F32)
    shifts[...] = jnp.concatenate([high, shift - high, padding], axis=0).astype(BF16)
    offset = dot_t(shifts[...], hw_ref[...])
    for copy in (hb_copy, std_copy, mean_copy):
        copy.wait()
    offset = offset[0:1] + offset[1:2] + hb_ref[...]
    repeats = outw // zch
    deviation = jnp.concatenate([std_ref[...]] * repeats, axis=1)
    average = jnp.concatenate([mean_ref[...]] * repeats, axis=1)
    projected = dot_t(centred[...], scaled[...]) * jnp.concatenate(factors, axis=0) + offset
    projected = projected * deviation + average
    strip[0:8, :] = jnp.zeros((8, 128), F32)
    strip[8 : 8 + cols, :] = jnp.concatenate([projected[0:cols], projected[cols:rows]], axis=1)
    strip[8 + cols :, :] = jnp.zeros((strip.shape[0] - 8 - cols, 128), F32)
    for side in range(widths):
        lat[side] = strip[7 + side * pw : 7 + side * pw + CP, :].astype(BF16)

    def targets():
        for k in range(4):
            for side in range(widths):
                to_ha = 2 * pp - 1 + k
                valid = (to_ha >= 0) & (to_ha < heights)
                mine = (to_ha == ha) & (wa == side)
                kind = 0 if k in (1, 2) else 1
                copy = pltpu.make_async_remote_copy(
                    src_ref=lat.at[side],
                    dst_ref=recv.at[frame, kind],
                    send_sem=send_sem.at[k, side],
                    recv_sem=recv_sem.at[frame, kind],
                    device_id={"ha": to_ha, "wa": side},
                    device_id_type=MESH,
                )
                yield k, valid, mine, copy, side, kind

    expected = jnp.int32(1)
    for _, valid, mine, _, _, _ in targets():
        expected += jnp.where(valid & jnp.logical_not(mine), 1, 0)
    pl.semaphore_wait(barrier, expected)
    lead = (frame == F - 1) & (pp == 0)

    @pl.when((frame == F - 1) & (pp == 1))
    def _():
        pl.semaphore_wait(turn_sem, 1)

    for k, valid, mine, copy, side, kind in targets():
        if k == 2 and side == 0:
            @pl.when(lead)
            def _():
                pl.semaphore_signal(
                    turn_sem, inc=1, device_id={"wa": 1 - wa}, device_id_type=MESH
                )

        @pl.when(valid & jnp.logical_not(mine))
        def _():
            copy.start()

        @pl.when(valid & mine)
        def _():
            recv[frame, kind] = lat[side]

    w_send.start()

    for copy in (ciw_copy, cib_copy, gain_copy):
        copy.wait()
    wc[...] = jnp.zeros(wc.shape, BF16)
    for a in range(3):
        for win_row in range(4):
            for win_col in range(4):
                k0 = a * 256 + (win_col // 2) * 128 + (win_row // 2) * 64
                k0 += ((win_row % 2) * 2 + win_col % 2) * zch
                for o_row in range(2):
                    for o_col in range(2):
                        b, e = win_row - o_row, win_col - o_col
                        if 0 <= b < 3 and 0 <= e < 3:
                            r0 = ((3 * a + b) * 3 + e) * zch
                            c0 = (o_row * 2 + o_col) * chan
                            wc[k0 : k0 + zch, c0 : c0 + chan] = ciw_ref[r0 : r0 + zch, :]

    zbuf[...] = jnp.zeros(zbuf.shape, F32)
    lane = lax.broadcasted_iota(jnp.int32, (CP, 128), 1)
    own_lane = (lane < 64) ^ (odd == 1)
    position = lax.broadcasted_iota(jnp.int32, (CP, 1), 0)
    bias_in = jnp.concatenate([cib_ref[...]] * 4, axis=1)
    gain = gain_ref[...]

    def take(ff):
        for kind in range(2):
            device, exists = source(ff, kind)

            @pl.when(exists & (device != me))
            def _():
                pltpu.make_async_remote_copy(
                    src_ref=lat.at[0],
                    dst_ref=recv.at[ff, kind],
                    send_sem=send_sem.at[0, 0],
                    recv_sem=recv_sem.at[ff, kind],
                    device_id={"wa": 1 - wa},
                    device_id_type=MESH,
                ).wait_recv()

    def windows(ff):
        near = recv[ff, 0].astype(F32)
        mixed = jnp.where(own_lane, near, recv[ff, 1].astype(F32))
        mixed = jnp.concatenate([mixed[:, 64:128], mixed[:, 0:64]], axis=1)
        for i in range(2):
            dense = jnp.where(odd == 1 - i, near, mixed)
            zbuf[i, 0:CP, :] = dense
            pair[ff, i, :, 0:128] = dense.astype(BF16)
            pair[ff, i, :, 128:256] = zbuf[i, 1 : 1 + CP, :].astype(BF16)

    tall = 2 * CP

    def activate(ff):
        base = ff * tall
        for i in range(2):
            for o_row in range(2):
                row = 2 * i + o_row
                for o_col in range(2):
                    c0 = (o_row * 2 + o_col) * chan
                    v = ybuf[base + i * CP : base + (i + 1) * CP, c0 : c0 + chan]
                    factor = lax.rsqrt(jnp.mean(v * v, axis=-1, keepdims=True) + 1e-06)
                    if o_col == 0:
                        keep = (position > 0) | (wa > 0)
                    else:
                        keep = (position < pw) | (wa < widths - 1)
                    if row == 0:
                        keep = keep & (ha > 0)
                    if row == 3:
                        keep = keep & (ha < heights - 1)
                    half = v * jnp.where(keep, 0.5 * factor, 0.0) * gain
                    xbuf[o_col] = half * jnp.tanh(half) + half
                x0 = xbuf[0, 0:pw, :]
                x1 = xbuf[1, 0:pw, :]
                x0s = xbuf[0, 1 : 1 + pw, :]
                x1s = xbuf[1, 1 : 1 + pw, :]
                act[ff, row, :, 0:chan] = jnp.concatenate([x0, x1], axis=0).astype(BF16)
                act[ff, row, :, chan : 2 * chan] = jnp.concatenate([x1, x0s], axis=0).astype(BF16)
                act[ff, row, :, 2 * chan : 3 * chan] = jnp.concatenate([x0s, x1s], axis=0).astype(
                    BF16
                )
                if row in (1, 2):
                    c0 = o_row * 2 * chan
                    c1 = c0 + chan
                    r0 = base + i * CP
                    even = ybuf[r0 : r0 + pw, c1 : c1 + chan]
                    after = ybuf[r0 + 1 : r0 + 1 + pw, c0:c1]
                    for q in range(chan // 128):
                        part = slice(q * 128, q * 128 + 128)
                        stage[q, pl.ds(0, pw, stride=2), :] = even[:, part]
                        stage[q, pl.ds(1, pw, stride=2), :] = after[:, part]
                        blk[ff, row - 1, :, part] = stage[q].astype(BF16)

    def block_of(ff):
        return pair[ff].reshape(tall, 256)

    def rounded(ff, total):
        ybuf[ff * tall : (ff + 1) * tall, :] = total.astype(BF16).astype(F32)

    def by_taps(lhs, lo):
        return jnp.dot(lhs, wc[lo : lo + lhs.shape[1], :], preferred_element_type=F32)

    take(0)
    windows(0)
    rounded(0, by_taps(block_of(0), 512) + bias_in)
    activate(0)
    take(1)
    windows(1)
    lhs = jnp.concatenate([block_of(0), block_of(1)], axis=1)
    rounded(1, by_taps(lhs, 256) + bias_in)
    activate(1)
    take(2)
    windows(2)
    blank = jnp.zeros((tall, 256), BF16)
    lines = [(block_of(0), block_of(1), block_of(2)), (block_of(1), block_of(2), blank)]
    lhs = jnp.concatenate([jnp.concatenate(line, axis=1) for line in lines], axis=0)
    total = by_taps(lhs, 0) + bias_in
    rounded(2, total[0:tall])
    ybuf[3 * tall :, :] = total[tall:]
    activate(2)
    take(3)
    windows(3)
    rounded(3, ybuf[3 * tall :, :] + by_taps(block_of(3), 512))
    activate(3)

    for k, valid, mine, copy, _, _ in targets():
        pending = valid & jnp.logical_not(mine)

        @pl.when(pending)
        def _():
            copy.wait_send()

    w_copy.wait()
    w_send.wait()


def convolve(act, w_ref, blk, cb_ref, out1, out2, acc, stage, res, sem):
    frames, _, cols, depth = act.shape
    chan = w_ref.shape[0]
    pw = cols // 2
    shortcut = pltpu.make_async_copy(blk, out1, sem.at[0])
    shortcut.start()
    block = 2 * cols
    split = 256
    rest = chan - split

    def lhs(count):
        parts = [act[0:count, b : b + 2].reshape(count * block, depth) for b in range(3)]
        return jnp.concatenate(parts, axis=1)

    def taps(a, lo, hi):
        return w_ref[lo:hi, 3 * a * depth : 3 * (a + 1) * depth]

    acc[:, 0:split] = dot_t(lhs(4), taps(2, 0, split))
    both = dot_t(lhs(4), jnp.concatenate([taps(2, split, chan), taps(1, 0, rest)], axis=0))
    acc[:, split:chan] = both[:, 0:rest]
    acc[block:, 0:rest] += both[0 : 3 * block, rest : 2 * rest]
    acc[block:, rest:chan] += dot_t(lhs(3), taps(1, rest, chan))
    bias = cb_ref[...].reshape(1, chan)
    copies = [shortcut]

    def finish(ff):
        for row in range(2):
            r0 = (2 * ff + row) * cols
            full = acc[r0 : r0 + cols, :] + bias
            for q in range(chan // 128):
                part = slice(q * 128, q * 128 + 128)
                stage[q, pl.ds(0, pw, stride=2), :] = full[0:pw, part]
                stage[q, pl.ds(1, pw, stride=2), :] = full[pw:cols, part]
                res[ff, row, :, part] = stage[q].astype(BF16)
        copy = pltpu.make_async_copy(res.at[ff], out2.at[ff], sem.at[1 + ff])
        copy.start()
        copies.append(copy)

    late = dot_t(lhs(2), taps(0, 0, split))
    acc[2 * block :, split:chan] += dot_t(lhs(2), taps(0, split, chan))
    finish(0)
    finish(1)
    acc[2 * block :, 0:split] += late
    finish(2)
    finish(3)
    for copy in copies:
        copy.wait()


def shards(
    tokens,
    timestep,
    time_table,
    modulation,
    head_weight,
    head_bias,
    latent_std,
    latent_mean,
    conv_in_weight,
    conv_in_bias,
    norm_gain,
    conv_weight,
    conv_bias,
):
    heights = lax.axis_size("ha")
    widths = lax.axis_size("wa")
    rows, width = tokens.shape
    cols = rows // 2
    chan = norm_gain.shape[0]
    hbm = pl.BlockSpec(memory_space=pltpu.HBM)
    vmem = pl.BlockSpec(memory_space=pltpu.VMEM)
    out = jax.ShapeDtypeStruct((F, 2, cols, chan), BF16)
    inner = pl.pallas_call(
        functools.partial(prepare, heights, widths),
        out_shape=(
            pltpu.VMEM((F, 4, cols, 3 * chan), BF16),
            pltpu.VMEM((chan, conv_weight.shape[0]), BF16),
            pltpu.VMEM((F, 2, cols, chan), BF16),
        ),
        in_specs=[hbm] * 12,
        out_specs=(vmem, vmem, vmem),
        scratch_shapes=[
            pltpu.VMEM((rows, width), BF16),
            pltpu.SMEM((1,), jnp.int32),
            pltpu.VMEM(time_table.shape, F32),
            pltpu.VMEM(modulation.shape, F32),
            pltpu.VMEM(head_weight.shape[::-1], BF16),
            pltpu.VMEM((1,) + head_bias.shape, F32),
            pltpu.VMEM((1,) + latent_std.shape, F32),
            pltpu.VMEM((1,) + latent_mean.shape, F32),
            pltpu.VMEM(conv_in_weight.shape, BF16),
            pltpu.VMEM((1, chan), F32),
            pltpu.VMEM((1, chan), F32),
            pltpu.VMEM(head_weight.shape[::-1], BF16),
            pltpu.VMEM((16, width), BF16),
            pltpu.VMEM((rows, width), BF16),
            pltpu.VMEM((cols + 24, 128), F32),
            pltpu.VMEM((widths, CP, 128), BF16),
            pltpu.VMEM((F, 2, CP, 128), BF16),
            pltpu.VMEM((2, CP + 8, 128), F32),
            pltpu.VMEM((F, 2, CP, 256), BF16),
            pltpu.VMEM((768, 4 * chan), BF16),
            pltpu.VMEM((F * 2 * CP, 4 * chan), F32),
            pltpu.VMEM((2, CP, chan), F32),
            pltpu.VMEM((chan // 128, cols, 128), F32),
            pltpu.SemaphoreType.DMA((rows // CHUNK,)),
            pltpu.SemaphoreType.DMA((11,)),
            pltpu.SemaphoreType.DMA((4, widths)),
            pltpu.SemaphoreType.DMA((F, 2)),
            pltpu.SemaphoreType.DMA((2,)),
            pltpu.SemaphoreType.REGULAR,
        ],
        compiler_params=pltpu.CompilerParams(
            collective_id=0, has_side_effects=True, vmem_limit_bytes=48 << 20
        ),
    )(
        *(
            x if x is timestep else pltpu.with_memory_space_constraint(x, pltpu.HBM)
            for x in (
                tokens,
                timestep,
                time_table,
                modulation,
                head_weight.T,
                head_bias,
                latent_std,
                latent_mean,
                conv_in_weight,
                conv_in_bias,
                norm_gain,
                conv_weight.T,
            )
        )
    )
    return tuple(
        pl.pallas_call(
            convolve,
            out_shape=(out, out),
            in_specs=[vmem] * 4,
            out_specs=(hbm, hbm),
            scratch_shapes=[
                pltpu.VMEM((F * 2 * cols, chan), F32),
                pltpu.VMEM((chan // 128, cols, 128), F32),
                pltpu.VMEM((F, 2, cols, chan), BF16),
                pltpu.SemaphoreType.DMA((1 + F,)),
            ],
            compiler_params=pltpu.CompilerParams(vmem_limit_bytes=32 << 20),
        )(*inner, conv_bias)
    )


def solution(mesh):
    in_specs = (
        P(("clips", "ha", "wa"), None),
        P("clips"),
        P(),
        P(),
        P(),
        P(),
        P(),
        P(),
        P(),
        P(),
        P(),
        P(None, "wa"),
        P(),
    )
    out_specs = (P("clips", "ha", "wa", None), P("clips", "ha", "wa", None))
    return jax.shard_map(shards, mesh=mesh, in_specs=in_specs, out_specs=out_specs, check_vma=False)
```

```python
import functools

import jax
import jax.numpy as jnp
from jax import lax
from jax.experimental import pallas as pl
from jax.experimental.pallas import tpu as pltpu
from jax.sharding import PartitionSpec as P

F = 4
MESH = pl.DeviceIdType.MESH
CP = 48
F32 = jnp.float32
BF16 = jnp.bfloat16
CHUNK = 32


def dot_t(lhs, rhs):
    return lax.dot_general(lhs, rhs, (((1,), (1,)), ((), ())), preferred_element_type=F32)


def prepare(
    heights,
    widths,
    tok_hbm,
    ts_hbm,
    table_hbm,
    mod_hbm,
    hw_hbm,
    hb_hbm,
    std_hbm,
    mean_hbm,
    ciw_hbm,
    cib_hbm,
    gain_hbm,
    w_hbm,
    act,
    w_ref,
    blk,
    tok,
    ts_ref,
    table_ref,
    mod_ref,
    hw_ref,
    hb_ref,
    std_ref,
    mean_ref,
    ciw_ref,
    cib_ref,
    gain_ref,
    scaled,
    shifts,
    centred,
    strip,
    lat,
    recv,
    zbuf,
    pair,
    wc,
    ybuf,
    xbuf,
    stage,
    tok_sem,
    in_sem,
    send_sem,
    recv_sem,
    w_sem,
    turn_sem,
):
    ha = lax.axis_index("ha")
    wa = lax.axis_index("wa")
    me = ha * widths + wa
    quarter = heights * widths // F
    frame = me // quarter
    pp = me % quarter
    rows = tok.shape[0]
    cols = rows // 2
    pw = cols // widths
    chan = gain_ref.shape[1]
    half_chan = w_hbm.shape[0]
    zch = std_ref.shape[1]
    odd = ha % 2

    def tok_copy(i):
        part = pl.ds(pl.multiple_of(i * CHUNK, CHUNK), CHUNK)
        return pltpu.make_async_copy(tok_hbm.at[part], tok.at[part], tok_sem.at[i])

    my_half = pl.ds(pl.multiple_of(wa * half_chan, 64), half_chan)
    ts_copy = pltpu.make_async_copy(ts_hbm, ts_ref, in_sem.at[0])
    table_copy = pltpu.make_async_copy(table_hbm, table_ref, in_sem.at[1])
    mod_copy = pltpu.make_async_copy(mod_hbm, mod_ref, in_sem.at[2])
    hw_copy = pltpu.make_async_copy(hw_hbm, hw_ref, in_sem.at[3])
    hb_copy = pltpu.make_async_copy(hb_hbm, hb_ref.at[0], in_sem.at[4])
    std_copy = pltpu.make_async_copy(std_hbm, std_ref.at[0], in_sem.at[5])
    mean_copy = pltpu.make_async_copy(mean_hbm, mean_ref.at[0], in_sem.at[6])
    ciw_copy = pltpu.make_async_copy(ciw_hbm, ciw_ref, in_sem.at[7])
    cib_copy = pltpu.make_async_copy(cib_hbm, cib_ref.at[0], in_sem.at[8])
    gain_copy = pltpu.make_async_copy(gain_hbm, gain_ref.at[0], in_sem.at[9])
    w_copy = pltpu.make_async_copy(w_hbm, w_ref.at[my_half], in_sem.at[10])
    w_send = pltpu.make_async_remote_copy(
        src_ref=w_hbm,
        dst_ref=w_ref.at[my_half],
        send_sem=w_sem.at[0],
        recv_sem=w_sem.at[1],
        device_id={"wa": 1 - wa},
        device_id_type=MESH,
    )
    for i in range(rows // CHUNK):
        tok_copy(i).start()
    for copy in (ts_copy, mod_copy):
        copy.start()

    def source(ff, kind):
        if kind == 0:
            return ff * quarter + ha // 2, ha >= 0
        beside = ha + 2 * odd - 1
        return ff * quarter + ha // 2 + 2 * odd - 1, (beside >= 0) & (beside < heights)

    @pl.when((ha == 0) | (ha == heights - 1))
    def _():
        for ff in range(F):
            recv[ff, 1] = jnp.zeros(recv.shape[2:], BF16)

    barrier = pltpu.get_barrier_semaphore()
    for ff in range(F):
        for kind in range(2):
            device, exists = source(ff, kind)

            @pl.when(exists & (device != me))
            def _():
                pl.semaphore_signal(
                    barrier,
                    inc=1,
                    device_id={"ha": device // widths, "wa": device % widths},
                    device_id_type=MESH,
                )

    pl.semaphore_signal(barrier, inc=1, device_id={"wa": 1 - wa}, device_id_type=MESH)

    for copy in (hw_copy, table_copy, hb_copy, std_copy, mean_copy):
        copy.start()
    factors = []
    for i in range(rows // CHUNK):
        tok_copy(i).wait()
    for i in range(rows // CHUNK):
        part = slice(i * CHUNK, (i + 1) * CHUNK)
        values = tok[part, :].astype(F32)
        centre = jnp.mean(values, axis=-1, keepdims=True)
        delta = values - centre
        spread = jnp.mean(delta * delta, axis=-1, keepdims=True)
        centred[part, :] = delta.astype(BF16)
        factors.append(lax.rsqrt(spread + 1e-06))

    for copy in (ts_copy, mod_copy, table_copy, hw_copy):
        copy.wait()
    for copy in (ciw_copy, cib_copy, gain_copy, w_copy):
        copy.start()
    embed = table_ref[pl.ds(ts_ref[0], 1), :]
    shift = mod_ref[0:1, :] + embed
    scale = 1.0 + (mod_ref[1:2, :] + embed)
    outw = hw_ref.shape[0]
    for i in range(outw // 16):
        part = slice(i * 16, (i + 1) * 16)
        scaled[part, :] = (hw_ref[part, :].astype(F32) * scale).astype(BF16)
    high = shift.astype(BF16).astype(F32)
    padding = jnp.zeros((14, shift.shape[1]), F32)
    shifts[...] = jnp.concatenate([high, shift - high, padding], axis=0).astype(BF16)
    offset = dot_t(shifts[...], hw_ref[...])
    for copy in (hb_copy, std_copy, mean_copy):
        copy.wait()
    offset = offset[0:1] + offset[1:2] + hb_ref[...]
    repeats = outw // zch
    deviation = jnp.concatenate([std_ref[...]] * repeats, axis=1)
    average = jnp.concatenate([mean_ref[...]] * repeats, axis=1)
    projected = dot_t(centred[...], scaled[...]) * jnp.concatenate(factors, axis=0) + offset
    projected = projected * deviation + average
    strip[0:8, :] = jnp.zeros((8, 128), F32)
    strip[8 : 8 + cols, :] = jnp.concatenate([projected[0:cols], projected[cols:rows]], axis=1)
    strip[8 + cols :, :] = jnp.zeros((strip.shape[0] - 8 - cols, 128), F32)
    for side in range(widths):
        lat[side] = strip[7 + side * pw : 7 + side * pw + CP, :].astype(BF16)

    def targets():
        for k in range(4):
            for side in range(widths):
                to_ha = 2 * pp - 1 + k
                valid = (to_ha >= 0) & (to_ha < heights)
                mine = (to_ha == ha) & (wa == side)
                kind = 0 if k in (1, 2) else 1
                copy = pltpu.make_async_remote_copy(
                    src_ref=lat.at[side],
                    dst_ref=recv.at[frame, kind],
                    send_sem=send_sem.at[k, side],
                    recv_sem=recv_sem.at[frame, kind],
                    device_id={"ha": to_ha, "wa": side},
                    device_id_type=MESH,
                )
                yield k, valid, mine, copy, side, kind

    expected = jnp.int32(1)
    for _, valid, mine, _, _, _ in targets():
        expected += jnp.where(valid & jnp.logical_not(mine), 1, 0)
    pl.semaphore_wait(barrier, expected)
    lead = (frame == F - 1) & (pp == 0)

    @pl.when((frame == F - 1) & (pp == 1))
    def _():
        pl.semaphore_wait(turn_sem, 1)

    for k, valid, mine, copy, side, kind in targets():
        if k == 2 and side == 0:
            @pl.when(lead)
            def _():
                pl.semaphore_signal(
                    turn_sem, inc=1, device_id={"wa": 1 - wa}, device_id_type=MESH
                )

        @pl.when(valid & jnp.logical_not(mine))
        def _():
            copy.start()

        @pl.when(valid & mine)
        def _():
            recv[frame, kind] = lat[side]

    w_send.start()

    for copy in (ciw_copy, cib_copy, gain_copy):
        copy.wait()
    wc[...] = jnp.zeros(wc.shape, BF16)
    for a in range(3):
        for win_row in range(4):
            for win_col in range(4):
                k0 = a * 256 + (win_col // 2) * 128 + (win_row // 2) * 64
                k0 += ((win_row % 2) * 2 + win_col % 2) * zch
                for o_row in range(2):
                    for o_col in range(2):
                        b, e = win_row - o_row, win_col - o_col
                        if 0 <= b < 3 and 0 <= e < 3:
                            r0 = ((3 * a + b) * 3 + e) * zch
                            c0 = (o_row * 2 + o_col) * chan
                            wc[k0 : k0 + zch, c0 : c0 + chan] = ciw_ref[r0 : r0 + zch, :]

    zbuf[...] = jnp.zeros(zbuf.shape, F32)
    lane = lax.broadcasted_iota(jnp.int32, (CP, 128), 1)
    own_lane = (lane < 64) ^ (odd == 1)
    position = lax.broadcasted_iota(jnp.int32, (CP, 1), 0)
    bias_in = jnp.concatenate([cib_ref[...]] * 4, axis=1)
    gain = gain_ref[...]

    def take(ff):
        for kind in range(2):
            device, exists = source(ff, kind)

            @pl.when(exists & (device != me))
            def _():
                pltpu.make_async_remote_copy(
                    src_ref=lat.at[0],
                    dst_ref=recv.at[ff, kind],
                    send_sem=send_sem.at[0, 0],
                    recv_sem=recv_sem.at[ff, kind],
                    device_id={"wa": 1 - wa},
                    device_id_type=MESH,
                ).wait_recv()

    def windows(ff):
        near = recv[ff, 0].astype(F32)
        mixed = jnp.where(own_lane, near, recv[ff, 1].astype(F32))
        mixed = jnp.concatenate([mixed[:, 64:128], mixed[:, 0:64]], axis=1)
        for i in range(2):
            dense = jnp.where(odd == 1 - i, near, mixed)
            zbuf[i, 0:CP, :] = dense
            pair[ff, i, :, 0:128] = dense.astype(BF16)
            pair[ff, i, :, 128:256] = zbuf[i, 1 : 1 + CP, :].astype(BF16)

    tall = 2 * CP

    def activate(ff):
        base = ff * tall
        for i in range(2):
            for o_row in range(2):
                row = 2 * i + o_row
                for o_col in range(2):
                    c0 = (o_row * 2 + o_col) * chan
                    v = ybuf[base + i * CP : base + (i + 1) * CP, c0 : c0 + chan]
                    factor = lax.rsqrt(jnp.mean(v * v, axis=-1, keepdims=True) + 1e-06)
                    if o_col == 0:
                        keep = (position > 0) | (wa > 0)
                    else:
                        keep = (position < pw) | (wa < widths - 1)
                    if row == 0:
                        keep = keep & (ha > 0)
                    if row == 3:
                        keep = keep & (ha < heights - 1)
                    half = v * jnp.where(keep, 0.5 * factor, 0.0) * gain
                    xbuf[o_col] = half * jnp.tanh(half) + half
                x0 = xbuf[0, 0:pw, :]
                x1 = xbuf[1, 0:pw, :]
                x0s = xbuf[0, 1 : 1 + pw, :]
                x1s = xbuf[1, 1 : 1 + pw, :]
                act[ff, row, :, 0:chan] = jnp.concatenate([x0, x1], axis=0).astype(BF16)
                act[ff, row, :, chan : 2 * chan] = jnp.concatenate([x1, x0s], axis=0).astype(BF16)
                act[ff, row, :, 2 * chan : 3 * chan] = jnp.concatenate([x0s, x1s], axis=0).astype(
                    BF16
                )
                if row in (1, 2):
                    c0 = o_row * 2 * chan
                    c1 = c0 + chan
                    r0 = base + i * CP
                    even = ybuf[r0 : r0 + pw, c1 : c1 + chan]
                    after = ybuf[r0 + 1 : r0 + 1 + pw, c0:c1]
                    for q in range(chan // 128):
                        part = slice(q * 128, q * 128 + 128)
                        stage[q, pl.ds(0, pw, stride=2), :] = even[:, part]
                        stage[q, pl.ds(1, pw, stride=2), :] = after[:, part]
                        blk[ff, row - 1, :, part] = stage[q].astype(BF16)

    def block_of(ff):
        return pair[ff].reshape(tall, 256)

    def rounded(ff, total):
        ybuf[ff * tall : (ff + 1) * tall, :] = total.astype(BF16).astype(F32)

    def by_taps(lhs, lo):
        return jnp.dot(lhs, wc[lo : lo + lhs.shape[1], :], preferred_element_type=F32)

    take(0)
    windows(0)
    rounded(0, by_taps(block_of(0), 512) + bias_in)
    take(1)
    windows(1)
    lhs = jnp.concatenate([block_of(0), block_of(1)], axis=1)
    rounded(1, by_taps(lhs, 256) + bias_in)
    activate(0)
    take(2)
    windows(2)
    blank = jnp.zeros((tall, 256), BF16)
    lines = [(block_of(0), block_of(1), block_of(2)), (block_of(1), block_of(2), blank)]
    lhs = jnp.concatenate([jnp.concatenate(line, axis=1) for line in lines], axis=0)
    total = by_taps(lhs, 0) + bias_in
    rounded(2, total[0:tall])
    ybuf[3 * tall :, :] = total[tall:]
    activate(1)
    activate(2)
    take(3)
    windows(3)
    rounded(3, ybuf[3 * tall :, :] + by_taps(block_of(3), 512))
    activate(3)

    for k, valid, mine, copy, _, _ in targets():
        pending = valid & jnp.logical_not(mine)

        @pl.when(pending)
        def _():
            copy.wait_send()

    w_copy.wait()
    w_send.wait()


def convolve(act, w_ref, blk, cb_ref, out1, out2, acc, stage, res, sem):
    frames, _, cols, depth = act.shape
    chan = w_ref.shape[0]
    pw = cols // 2
    shortcut = pltpu.make_async_copy(blk, out1, sem.at[0])
    shortcut.start()
    block = 2 * cols
    split = 256
    rest = chan - split

    def lhs(count):
        parts = [act[0:count, b : b + 2].reshape(count * block, depth) for b in range(3)]
        return jnp.concatenate(parts, axis=1)

    def taps(a, lo, hi):
        return w_ref[lo:hi, 3 * a * depth : 3 * (a + 1) * depth]

    acc[:, 0:split] = dot_t(lhs(4), taps(2, 0, split))
    both = dot_t(lhs(4), jnp.concatenate([taps(2, split, chan), taps(1, 0, rest)], axis=0))
    acc[:, split:chan] = both[:, 0:rest]
    acc[block:, 0:rest] += both[0 : 3 * block, rest : 2 * rest]
    acc[block:, rest:chan] += dot_t(lhs(3), taps(1, rest, chan))
    bias = cb_ref[...].reshape(1, chan)
    copies = [shortcut]

    def finish(ff):
        for row in range(2):
            r0 = (2 * ff + row) * cols
            full = acc[r0 : r0 + cols, :] + bias
            for q in range(chan // 128):
                part = slice(q * 128, q * 128 + 128)
                stage[q, pl.ds(0, pw, stride=2), :] = full[0:pw, part]
                stage[q, pl.ds(1, pw, stride=2), :] = full[pw:cols, part]
                res[ff, row, :, part] = stage[q].astype(BF16)
        copy = pltpu.make_async_copy(res.at[ff], out2.at[ff], sem.at[1 + ff])
        copy.start()
        copies.append(copy)

    late = dot_t(lhs(2), taps(0, 0, split))
    acc[2 * block :, split:chan] += dot_t(lhs(2), taps(0, split, chan))
    finish(0)
    finish(1)
    acc[2 * block :, 0:split] += late
    finish(2)
    finish(3)
    for copy in copies:
        copy.wait()


def shards(
    tokens,
    timestep,
    time_table,
    modulation,
    head_weight,
    head_bias,
    latent_std,
    latent_mean,
    conv_in_weight,
    conv_in_bias,
    norm_gain,
    conv_weight,
    conv_bias,
):
    heights = lax.axis_size("ha")
    widths = lax.axis_size("wa")
    rows, width = tokens.shape
    cols = rows // 2
    chan = norm_gain.shape[0]
    hbm = pl.BlockSpec(memory_space=pltpu.HBM)
    vmem = pl.BlockSpec(memory_space=pltpu.VMEM)
    out = jax.ShapeDtypeStruct((F, 2, cols, chan), BF16)
    inner = pl.pallas_call(
        functools.partial(prepare, heights, widths),
        out_shape=(
            pltpu.VMEM((F, 4, cols, 3 * chan), BF16),
            pltpu.VMEM((chan, conv_weight.shape[0]), BF16),
            pltpu.VMEM((F, 2, cols, chan), BF16),
        ),
        in_specs=[hbm] * 12,
        out_specs=(vmem, vmem, vmem),
        scratch_shapes=[
            pltpu.VMEM((rows, width), BF16),
            pltpu.SMEM((1,), jnp.int32),
            pltpu.VMEM(time_table.shape, F32),
            pltpu.VMEM(modulation.shape, F32),
            pltpu.VMEM(head_weight.shape[::-1], BF16),
            pltpu.VMEM((1,) + head_bias.shape, F32),
            pltpu.VMEM((1,) + latent_std.shape, F32),
            pltpu.VMEM((1,) + latent_mean.shape, F32),
            pltpu.VMEM(conv_in_weight.shape, BF16),
            pltpu.VMEM((1, chan), F32),
            pltpu.VMEM((1, chan), F32),
            pltpu.VMEM(head_weight.shape[::-1], BF16),
            pltpu.VMEM((16, width), BF16),
            pltpu.VMEM((rows, width), BF16),
            pltpu.VMEM((cols + 24, 128), F32),
            pltpu.VMEM((widths, CP, 128), BF16),
            pltpu.VMEM((F, 2, CP, 128), BF16),
            pltpu.VMEM((2, CP + 8, 128), F32),
            pltpu.VMEM((F, 2, CP, 256), BF16),
            pltpu.VMEM((768, 4 * chan), BF16),
            pltpu.VMEM((F * 2 * CP, 4 * chan), F32),
            pltpu.VMEM((2, CP, chan), F32),
            pltpu.VMEM((chan // 128, cols, 128), F32),
            pltpu.SemaphoreType.DMA((rows // CHUNK,)),
            pltpu.SemaphoreType.DMA((11,)),
            pltpu.SemaphoreType.DMA((4, widths)),
            pltpu.SemaphoreType.DMA((F, 2)),
            pltpu.SemaphoreType.DMA((2,)),
            pltpu.SemaphoreType.REGULAR,
        ],
        compiler_params=pltpu.CompilerParams(
            collective_id=0, has_side_effects=True, vmem_limit_bytes=48 << 20
        ),
    )(
        *(
            x if x is timestep else pltpu.with_memory_space_constraint(x, pltpu.HBM)
            for x in (
                tokens,
                timestep,
                time_table,
                modulation,
                head_weight.T,
                head_bias,
                latent_std,
                latent_mean,
                conv_in_weight,
                conv_in_bias,
                norm_gain,
                conv_weight.T,
            )
        )
    )
    return tuple(
        pl.pallas_call(
            convolve,
            out_shape=(out, out),
            in_specs=[vmem] * 4,
            out_specs=(hbm, hbm),
            scratch_shapes=[
                pltpu.VMEM((F * 2 * cols, chan), F32),
                pltpu.VMEM((chan // 128, cols, 128), F32),
                pltpu.VMEM((F, 2, cols, chan), BF16),
                pltpu.SemaphoreType.DMA((1 + F,)),
            ],
            compiler_params=pltpu.CompilerParams(vmem_limit_bytes=32 << 20),
        )(*inner, conv_bias)
    )


def solution(mesh):
    in_specs = (
        P(("clips", "ha", "wa"), None),
        P("clips"),
        P(),
        P(),
        P(),
        P(),
        P(),
        P(),
        P(),
        P(),
        P(),
        P(None, "wa"),
        P(),
    )
    out_specs = (P("clips", "ha", "wa", None), P("clips", "ha", "wa", None))
    return jax.shard_map(shards, mesh=mesh, in_specs=in_specs, out_specs=out_specs, check_vma=False)
```
